32 devices in a mesh: member: 8 (over z, y), region: 4 (over x, core).
Axes of the slice: x: 2, y: 2, z: 4, core: 2. Of those that a mesh axis runs over, the one named last changes fastest.
Arguments:
- background_realizations: float32 [1024, 32768], P('member', 'region'), may hold values from -6 to 6
- realization_expected_data: float32 [1024, 16384], P('member', 'region'), may hold values from -6 to 6
- departure_values: float32 [1024, 16384], P('member', 'region'), may hold values from -6 to 6
- instrument_dispersion: float32 [16384], P('region'), may hold values from 0.5 to 2
- window_piece_offsets: int32 [4, 9], P('region'), may hold values from 0 to 64, as said below
- window_data_pieces: int32 [4, 8, 4], P('region'), may hold values from 0 to 39, as said below
- neighbor_piece_ids: int32 [4, 2, 4], P('region'), may hold values from 0 to 31, as said below
- coupling_indicator: int32 [4, 64, 4], P('region'), may hold values 0 or 1
Outputs:
- analysis: float32 [1024, 32768], P('member', 'region')
The draws below stay inside these ranges and needn't reach their ends.
Inputs may be any that keep to these rules, and one draw needn't show every extreme that they name: `window_piece_offsets`: each row starts at 0, ends at 64 and rises by 1 or more at each entry; entry p lies within 3 of p * 8; in every row one patch spans exactly 14 blocks. `window_data_pieces`: entries index a region's extended observation blocks: 0 to 31 its own, then 4 received from the region before it, then 4 from the region after it; the 4 entries of a patch differ. `neighbor_piece_ids`: entries index the sending region's own observation blocks; the 4 entries of a row differ.
All inputs are finite; a program needn't handle non-finite values. No bound on the sum of `coupling_indicator` on one device may be relied on, other than what follows from the above.
Results may differ from the reference program's by a relative error of at most 0.0003.
Values sent between devices are 32-bit elements; how exact they have to be, the bound alone decides.
A program may use at most 128 MiB of HBM per device.

```python
import math
import jax
import jax.numpy as jnp
from jax import lax

REALIZATION_NUM = 1024
PIECE_LENGTH = 128
OBS_PER = 4
LOCAL = 512
BLK_DEV = 8
HALF = 3
SEGMENTS_AREA = 64
OBSERVED_PARTS = 32
HB = 4
EXT = 40
DOMAIN_NUMBER = 4
PATCHES = 8
N_REGION = 4


def distinct_rows(key, shape_lead, choices, keep):
    scores = jax.random.randint(key, shape_lead + (choices,), 0, 2 ** 20) * choices
    scores = scores + jnp.arange(choices).astype(jnp.int32)
    order = jnp.argsort(scores, axis=-1, stable=True)
    return order[..., :keep].astype(jnp.int32)


def draw_window_piece_offsets(key, part):
    first_key, second_key = jax.random.split(jax.random.fold_in(key, 11))
    offsets = jax.random.randint(first_key, (DOMAIN_NUMBER, PATCHES + 1), -HALF, HALF + 1)
    chosen_patch = jax.random.randint(second_key, (DOMAIN_NUMBER, 1), 1, PATCHES - 1)
    column = jnp.arange(PATCHES + 1)[None, :]
    offsets = jnp.where(column == chosen_patch, -HALF, offsets)
    offsets = jnp.where(column == chosen_patch + 1, HALF, offsets)
    offsets = jnp.where((column == 0) | (column == PATCHES), 0, offsets)
    return (column * BLK_DEV + offsets).astype(jnp.int32)


def draw_window_data_pieces(key, part):
    return distinct_rows(jax.random.fold_in(key, 23), (DOMAIN_NUMBER, PATCHES), EXT, OBS_PER)


def draw_neighbor_piece_ids(key, part):
    return distinct_rows(jax.random.fold_in(key, 37), (DOMAIN_NUMBER, 2), OBSERVED_PARTS, HB)


def with_ends(drawn, key, least, top_value):
    longest = drawn.shape.index(max(drawn.shape))
    spots = []
    for shift in (0, 1):
        where = [jax.random.randint(jax.random.fold_in(key, axis), (), 0, length) for axis, length in enumerate(drawn.shape)]
        where[longest] = (where[longest] + shift) % drawn.shape[longest]
        spots.append(tuple(where))
    return drawn.at[spots[0]].set(least).at[spots[1]].set(top_value)


def levels(own_key, shape, cuts, low, top_value):
    loudness = 1.0
    for dim, blocks in cuts:
        steps = jax.random.uniform(jax.random.fold_in(jax.random.fold_in(own_key, 6), dim), (blocks,), jnp.float32, low / len(cuts), top_value / len(cuts))
        loudness = loudness * jnp.repeat(jnp.exp(steps), shape[dim] // blocks).reshape((-1,) + (1,) * (len(shape) - 1 - dim))
    return loudness


def gaussian(key, dims, width, most, cuts=(), kind=jnp.bfloat16):
    values = jax.random.normal(key, dims, jnp.float32) * width
    if len(cuts) > 0:
        values = levels(key, dims, cuts, -0.22, 0.18) * values
    return jnp.clip(values, min=-most, max=most).astype(kind)


def setup_inputs(seed: int = 0) -> dict:
    arg_keys = jax.random.split(jax.random.key(seed), 9)
    background_realizations = gaussian(arg_keys[0], (REALIZATION_NUM, DOMAIN_NUMBER * SEGMENTS_AREA * PIECE_LENGTH), 1.0, 6.0, ((0, 8), (1, 4)), jnp.float32)
    realization_expected_data = gaussian(arg_keys[1], (REALIZATION_NUM, DOMAIN_NUMBER * OBSERVED_PARTS * PIECE_LENGTH), 1.0, 6.0, ((0, 8), (1, 4)), jnp.float32)
    departure_values = gaussian(arg_keys[2], (REALIZATION_NUM, DOMAIN_NUMBER * OBSERVED_PARTS * PIECE_LENGTH), 1.0, 6.0, ((0, 8), (1, 4)), jnp.float32)
    instrument_dispersion = jnp.clip(jnp.exp(math.log(2.0) - 1.3862944 * jax.random.uniform(arg_keys[3], (DOMAIN_NUMBER * OBSERVED_PARTS * PIECE_LENGTH,), jnp.float32) ** levels(arg_keys[3], (DOMAIN_NUMBER * OBSERVED_PARTS * PIECE_LENGTH,), ((0, 4),), -0.2, 0.2)), 0.5, 2.0)
    window_piece_offsets = draw_window_piece_offsets(jax.random.fold_in(arg_keys[8], 71), 0)
    window_data_pieces = draw_window_data_pieces(jax.random.fold_in(arg_keys[8], 71), 0)
    neighbor_piece_ids = draw_neighbor_piece_ids(jax.random.fold_in(arg_keys[8], 71), 0)
    coupling_indicator = with_ends((jax.random.randint(arg_keys[7], (DOMAIN_NUMBER, SEGMENTS_AREA, OBS_PER), 0, 4) < 3).astype(jnp.int32), jax.random.fold_in(arg_keys[7], 1), 0, 1)
    return dict(background_realizations=background_realizations, realization_expected_data=realization_expected_data, departure_values=departure_values, instrument_dispersion=instrument_dispersion, window_piece_offsets=window_piece_offsets, window_data_pieces=window_data_pieces, neighbor_piece_ids=neighbor_piece_ids, coupling_indicator=coupling_indicator)


highest = lax.Precision.HIGHEST

def listed(stack, lists, axis_at):
    return jax.vmap(lambda region_data, region_list: jnp.take(region_data, region_list, axis=axis_at))(stack, lists)

def extended(stack, neighbor_piece_ids, axis_at):
    before = jnp.roll(listed(stack, neighbor_piece_ids[:, 0], axis_at), 1, axis=0)
    after = jnp.roll(listed(stack, neighbor_piece_ids[:, 1], axis_at), -1, axis=0)
    return jnp.concatenate([stack, before, after], axis=axis_at + 1)

def reference(background_realizations, realization_expected_data, departure_values, instrument_dispersion, window_piece_offsets, window_data_pieces, neighbor_piece_ids, coupling_indicator):
    realization_records = REALIZATION_NUM
    domain_records = N_REGION
    sample_vectors = background_realizations.reshape(realization_records, domain_records, SEGMENTS_AREA, PIECE_LENGTH).transpose(1, 0, 2, 3)
    expected_data = realization_expected_data.reshape(realization_records, domain_records, OBSERVED_PARTS, PIECE_LENGTH).transpose(1, 0, 2, 3)
    innovated = departure_values.reshape(realization_records, domain_records, OBSERVED_PARTS, PIECE_LENGTH).transpose(1, 0, 2, 3)
    variance = instrument_dispersion.reshape(domain_records, OBSERVED_PARTS, PIECE_LENGTH)
    pred_ext = extended(expected_data, neighbor_piece_ids, 1)
    innov_ext = extended(innovated, neighbor_piece_ids, 1)
    var_ext = extended(variance, neighbor_piece_ids, 0)

    def one_region(inputs):
        states, pred_region, innov_region, var_region, bounds_row, lists_row, cover_rows = inputs
        centred = states - jnp.mean(states, axis=0, keepdims=True)

        def solve_patch(chosen):
            raw = jnp.take(pred_region, chosen, axis=1).reshape(realization_records, LOCAL)
            perturbed = raw - jnp.mean(raw, axis=0, keepdims=True)
            local_innov = jnp.take(innov_region, chosen, axis=1).reshape(realization_records, LOCAL)
            local_var = jnp.take(var_region, chosen, axis=0).reshape(LOCAL)
            cov_obs = jnp.dot(perturbed.T.astype(jnp.float32), perturbed.astype(jnp.float32), precision=highest, preferred_element_type=jnp.float32) / (realization_records - 1.0)
            cov_obs = cov_obs + jnp.diag(local_var)
            factor = jnp.linalg.cholesky(cov_obs)
            weights = jax.scipy.linalg.cho_solve((factor, True), local_innov.T)
            return (perturbed, weights)
        perts, weights_all = lax.map(solve_patch, lists_row)
        block_ids = jnp.arange(SEGMENTS_AREA).astype(jnp.int32)
        owners = jnp.sum((bounds_row[None, 1:-1] <= block_ids[:, None]).astype(jnp.int32), axis=1)

        def one_block(block_inputs):
            column, owner_id, mark_row = block_inputs
            perturbed = perts[owner_id]
            weights = weights_all[owner_id]
            kalman_gain = jnp.dot(column.T.astype(jnp.float32), perturbed.astype(jnp.float32), precision=highest, preferred_element_type=jnp.float32) / (realization_records - 1.0)
            kalman_gain = kalman_gain * jnp.repeat(mark_row.astype(jnp.float32), PIECE_LENGTH)[None, :]
            return jnp.dot(weights.T.astype(jnp.float32), kalman_gain.T.astype(jnp.float32), precision=highest, preferred_element_type=jnp.float32)
        increments = lax.map(one_block, (centred.transpose(1, 0, 2), owners, cover_rows))
        return states + increments.transpose(1, 0, 2)
    analysed = lax.map(one_region, (sample_vectors, pred_ext, innov_ext, var_ext, window_piece_offsets, window_data_pieces, coupling_indicator))
    return analysed.transpose(1, 0, 2, 3).reshape(realization_records, domain_records * SEGMENTS_AREA * PIECE_LENGTH)
```

```python
import functools

import jax
import jax.numpy as jnp
from jax import lax
from jax.experimental import pallas as pl
from jax.experimental.pallas import tpu as pltpu
from jax.sharding import PartitionSpec as P

PIECE = 128
OBS_PER = 4
LOCAL = OBS_PER * PIECE
TILE = 256

MESH = pl.DeviceIdType.MESH
highest = lax.Precision.HIGHEST


def cols(start, count=1):
    return pl.ds(pl.multiple_of(start * PIECE, PIECE), count * PIECE)


def dot(left, right, contract, precision=None):
    return lax.dot_general(
        left,
        right,
        ((contract[0], contract[1]), ((), ())),
        precision=precision,
        preferred_element_type=jnp.float32,
    )


def at_least(value, bound):
    return jnp.clip(value - bound + 1, 0, 1).astype(jnp.float32)


PLAIN = ((1,), (0,))
BY_ROWS = ((1,), (1,))


def split(value):
    top = value.astype(jnp.bfloat16)
    return top, (value - top.astype(jnp.float32)).astype(jnp.bfloat16)


def factor_block(block, work_ref):
    size = block.shape[0]
    wide = 2 * size
    eye = lax.broadcasted_iota(jnp.int32, (size, size), 0) == lax.broadcasted_iota(
        jnp.int32, (size, size), 1
    )
    work_ref[:, :size] = block
    work_ref[:, size:] = eye.astype(jnp.float32)
    step_rows = 8
    row_ids = lax.broadcasted_iota(jnp.int32, (step_rows, wide), 0)
    for start in range(0, size, step_rows):
        rows = work_ref[start : start + step_rows, :]
        for j in range(step_rows):
            column = rows[:, start + j : start + j + 1]
            scale = 1.0 / jnp.sqrt(column[j : j + 1, :])
            pivot = rows[j : j + 1, :] * scale
            lowered = rows - (column * scale) * pivot
            rows = jnp.where(row_ids > j, lowered, jnp.where(row_ids == j, pivot, rows))
        work_ref[start : start + step_rows, :] = rows
        after = start + step_rows
        if after < size:
            change = dot(rows[:, :size], rows, ((0,), (0,)), highest)
            work_ref[after:, :] = work_ref[after:, :] - change[after:, :]


def snake(index, row, flip):
    return index + (index // row + flip) % 2 * (row - 1 - 2 * (index % row))


def analysis_kernel(
    plan,
    lists_ref,
    ids_ref,
    offsets_ref,
    cover_ref,
    background,
    expected_hbm,
    innov_hbm,
    own_var,
    out,
    expected,
    innov,
    own_e,
    own_d,
    ext_e,
    ext_d,
    ext_var,
    halo_send,
    var_send,
    pack,
    obs,
    devs,
    states,
    turned,
    turned_top,
    turned_low,
    trailing,
    work,
    inverses,
    panels,
    weight_top,
    weight_low,
    gain_top,
    gain_low,
    state_top,
    state_low,
    result,
    edge_inc,
    edge_got,
    member_send,
    member_recv,
    pair_send,
    pair_recv,
    halo_send_sem,
    halo_recv_sem,
    local_sem,
):
    groups, regions, row, per_device, spread = plan
    rows = expected.shape[0]
    own_count = expected.shape[1] // PIECE
    side = ids_ref.shape[1]
    members = groups * rows
    edge = spread * PIECE
    own_width = per_device * PIECE
    middle = own_width - 2 * edge
    me = lax.axis_index("member")
    region = lax.axis_index("region")
    flip = region % 2
    patch = snake(me, row, flip)
    has_dn = patch > 0
    has_up = patch < groups - 1
    member_dn = snake((patch + groups - 1) % groups, row, flip)
    member_up = snake((patch + 1) % groups, row, flip)
    region_after = (region + 1) % regions
    region_before = (region + regions - 1) % regions
    my_rows = pl.ds(pl.multiple_of(me * rows, rows), rows)

    def rows_of(member):
        return pl.ds(pl.multiple_of(member * rows, rows), rows)

    load_e = pltpu.make_async_copy(expected_hbm, expected, local_sem.at[0])
    load_d = pltpu.make_async_copy(innov_hbm, innov, local_sem.at[1])
    load_e.start()
    load_d.start()

    barrier = pltpu.get_barrier_semaphore()
    for k in range(1, groups):
        pl.semaphore_signal(
            barrier, inc=1, device_id=((me + k) % groups, region), device_id_type=MESH
        )
    for other in (region_after, region_before):
        pl.semaphore_signal(barrier, inc=1, device_id=(me, other), device_id_type=MESH)
    pl.semaphore_wait(barrier, groups + 1)

    def state_copy(slot, start, width, k):
        target = (me + k) % groups
        source = snake(target, row, flip) * own_width + start
        return pltpu.make_async_remote_copy(
            src_ref=background.at[:, pl.ds(pl.multiple_of(source, PIECE), width)],
            dst_ref=states.at[my_rows, edge + start : edge + start + width],
            send_sem=member_send.at[slot, k],
            recv_sem=member_recv.at[slot, k],
            device_id=(target, region),
            device_id_type=MESH,
        )

    def state_own(slot, start, width):
        source = patch * own_width + start
        return pltpu.make_async_copy(
            background.at[:, pl.ds(pl.multiple_of(source, PIECE), width)],
            states.at[my_rows, edge + start : edge + start + width],
            member_recv.at[slot, 0],
        )

    def send_states(slot, start, width):
        @pl.loop(1, groups)
        def _(k):
            state_copy(slot, start, width, k).start()

        state_own(slot, start, width).start()

    def take_states(slot, start, width):
        @pl.loop(1, groups)
        def _(k):
            state_copy(slot, start, width, k).wait_recv()

        state_own(slot, start, width).wait()

    def window_copy(slot, source, target_ref, k):
        return pltpu.make_async_remote_copy(
            src_ref=source.at[rows_of((me + k) % groups), :],
            dst_ref=target_ref.at[my_rows, :],
            send_sem=member_send.at[slot, k],
            recv_sem=member_recv.at[slot, k],
            device_id=((me + k) % groups, region),
            device_id_type=MESH,
        )

    def return_copy(slot, start, width, k):
        return pltpu.make_async_remote_copy(
            src_ref=result.at[rows_of((me + k) % groups), start : start + width],
            dst_ref=out.at[
                :, pl.ds(pl.multiple_of(patch * own_width + start, PIECE), width)
            ],
            send_sem=member_send.at[slot, k],
            recv_sem=member_recv.at[slot, k],
            device_id=((me + k) % groups, region),
            device_id_type=MESH,
        )

    def return_own(slot, start, width):
        return pltpu.make_async_copy(
            result.at[my_rows, start : start + width],
            out.at[:, pl.ds(pl.multiple_of(patch * own_width + start, PIECE), width)],
            member_recv.at[slot, 0],
        )

    def send_back(slot, start, width):
        @pl.loop(1, groups)
        def _(k):
            return_copy(slot, start, width, k).start()

        return_own(slot, start, width).start()

    S_MID, S_LOW, S_HIGH, W_E, W_D, R_MID, R_LOW, R_HIGH = range(8)
    pieces_of = {
        S_MID: (edge, middle),
        S_LOW: (0, edge),
        S_HIGH: (own_width - edge, edge),
    }

    for load, flat, own, ext in (
        (load_e, expected, own_e, ext_e),
        (load_d, innov, own_d, ext_d),
    ):
        load.wait()
        for n in range(own_count):
            block = flat[:, n * PIECE : (n + 1) * PIECE]
            own[n] = block
            ext[n] = block
    for n in range(own_count):
        ext_var[n] = own_var[n]
    halo_copies = []
    for part, (own, ext, send) in enumerate(
        ((own_e, ext_e, halo_send.at[0]), (own_var, ext_var, var_send), (own_d, ext_d, halo_send.at[1]))
    ):
        for way, other in ((0, region_after), (1, region_before)):
            for k in range(side):
                send[way, k] = own[ids_ref[way, k]]
            landing = own_count + way * side
            copy = pltpu.make_async_remote_copy(
                src_ref=send.at[way],
                dst_ref=ext.at[landing : landing + side],
                send_sem=halo_send_sem.at[part, way],
                recv_sem=halo_recv_sem.at[part, way],
                device_id=(me, other),
                device_id_type=MESH,
            )
            copy.start()
            halo_copies.append(copy)
    send_states(S_MID, *pieces_of[S_MID])

    def pack_window(ext, buffer, k):
        target = (me + k) % groups
        p = snake(target, row, flip)
        for n in range(OBS_PER):
            buffer[rows_of(target), n * PIECE : (n + 1) * PIECE] = ext[lists_ref[p, n]]

    for copy in halo_copies[:2]:
        copy.wait_recv()

    @pl.loop(1, groups)
    def _(k):
        pack_window(ext_e, pack.at[0], k)
        window_copy(W_E, pack.at[0], obs, k).start()

    pack_window(ext_e, obs, 0)
    for copy in halo_copies[2:]:
        copy.wait_recv()
    variances = [ext_var[lists_ref[patch, n]] for n in range(OBS_PER)]

    @pl.loop(1, groups)
    def _(k):
        pack_window(ext_d, pack.at[1], k)

    pack_window(ext_d, devs, 0)

    @pl.loop(1, groups)
    def _(k):
        window_copy(W_E, pack.at[0], obs, k).wait_send()
        window_copy(W_D, pack.at[1], devs, k).start()

    @pl.loop(1, groups)
    def _(k):
        window_copy(W_E, pack.at[0], obs, k).wait_recv()

    tiles = members // PIECE

    def add_rows(t, total):
        part = obs[pl.ds(pl.multiple_of(t * PIECE, PIECE), PIECE), :]
        return total + jnp.sum(part, axis=0, keepdims=True)

    mean = lax.fori_loop(0, tiles, add_rows, jnp.zeros((1, LOCAL), jnp.float32)) / members

    @pl.loop(0, tiles)
    def _(t):
        place = pl.ds(pl.multiple_of(t * PIECE, PIECE), PIECE)
        part = obs[place, :] - mean
        obs[place, :] = part
        flat = part.T
        turned[:, place] = flat
        top, low = split(flat)
        turned_top[:, place] = top
        turned_low[:, place] = low

    @pl.loop(0, LOCAL // TILE)
    def _(i):
        place = pl.ds(pl.multiple_of(i * TILE, TILE), TILE)

        @pl.loop(0, LOCAL // TILE)
        def _(j):
            other = pl.ds(pl.multiple_of(j * TILE, TILE), TILE)
            trailing[place, other] = dot(
                turned[place, :], obs[:, other], PLAIN, highest
            ) / (members - 1.0)

    eye = lax.broadcasted_iota(jnp.int32, (PIECE, PIECE), 0) == lax.broadcasted_iota(
        jnp.int32, (PIECE, PIECE), 1
    )
    for n in range(OBS_PER):
        place = slice(n * PIECE, (n + 1) * PIECE)
        trailing[place, place] = trailing[place, place] + jnp.where(eye, variances[n], 0.0)

    line = lax.broadcasted_iota(jnp.int32, (LOCAL, PIECE), 0)

    @pl.loop(0, OBS_PER)
    def _(k):
        place = cols(k)
        factor_block(trailing[place, place], work)

        @pl.when(k == 0)
        def _():
            send_states(S_LOW, *pieces_of[S_LOW])

        @pl.when(k == 2)
        def _():
            send_states(S_HIGH, *pieces_of[S_HIGH])

        inverse = work[:, PIECE:]
        inverses[place, :] = inverse
        panel = dot(trailing[:, place], inverse, BY_ROWS, highest)
        panel = jnp.where(line >= (k + 1) * PIECE, panel, 0.0)
        panels[:, place] = panel

        @pl.loop(0, LOCAL // PIECE)
        def _(i):
            part = cols(i)
            trailing[part, :] = trailing[part, :] - dot(
                panels[part, place], panels[:, place], BY_ROWS, highest
            )

    def forward(way):
        start, other = ((edge, member_dn), (own_width, member_up))[way]
        landing = (edge + own_width, 0)[way]
        return pltpu.make_async_remote_copy(
            src_ref=states.at[:, start : start + edge],
            dst_ref=states.at[:, landing : landing + edge],
            send_sem=pair_send.at[way],
            recv_sem=pair_recv.at[way],
            device_id=(other, region),
            device_id_type=MESH,
        )

    def backward(way):
        other = (member_up, member_dn)[way]
        return pltpu.make_async_remote_copy(
            src_ref=edge_inc.at[way],
            dst_ref=edge_got.at[way],
            send_sem=pair_send.at[2 + way],
            recv_sem=pair_recv.at[2 + way],
            device_id=(other, region),
            device_id_type=MESH,
        )

    take_states(S_LOW, *pieces_of[S_LOW])

    @pl.when(has_dn)
    def _():
        forward(0).start()

    @pl.loop(1, groups)
    def _(k):
        window_copy(W_D, pack.at[1], devs, k).wait_recv()

    @pl.loop(0, members // TILE)
    def _(t):
        place = pl.ds(pl.multiple_of(t * TILE, TILE), TILE)
        rest = devs[place, :]
        parts = []
        for k in range(OBS_PER):
            at = slice(k * PIECE, (k + 1) * PIECE)
            part = dot(rest[:, :PIECE], inverses[at, :], BY_ROWS, highest)
            parts.append(part)
            if k + 1 < OBS_PER:
                rest = rest[:, PIECE:] - dot(
                    part, panels[(k + 1) * PIECE :, at], BY_ROWS, highest
                )
        done = None
        for k in reversed(range(OBS_PER)):
            at = slice(k * PIECE, (k + 1) * PIECE)
            part = parts[k]
            if done is not None:
                part = part - dot(done, panels[(k + 1) * PIECE :, at], PLAIN, highest)
            part = dot(part, inverses[at, :], PLAIN, highest)
            done = part if done is None else jnp.concatenate([part, done], axis=1)
        top, low = split(done)
        weight_top[place, :] = top
        weight_low[place, :] = low

    blocks_total = cover_ref.shape[0]

    def find_gain(start, width):
        def add_states(t, total):
            part = states[
                pl.ds(pl.multiple_of(t * PIECE, PIECE), PIECE), start : start + width
            ]
            return total + jnp.sum(part, axis=0, keepdims=True)

        centre = (
            lax.fori_loop(0, tiles, add_states, jnp.zeros((1, width), jnp.float32))
            / members
        )

        @pl.loop(0, tiles)
        def _(t):
            place = pl.ds(pl.multiple_of(t * PIECE, PIECE), PIECE)
            top, low = split(states[place, start : start + width] - centre)
            state_top[place, :width] = top
            state_low[place, :width] = low

        first = patch * per_device - spread + start // PIECE

        @pl.loop(0, OBS_PER)
        def _(n):
            place = cols(n)
            left_top, left_low = turned_top[place, :], turned_low[place, :]
            right_top, right_low = state_top[:, :width], state_low[:, :width]
            gain = (
                dot(left_top, right_top, PLAIN)
                + dot(left_top, right_low, PLAIN)
                + dot(left_low, right_top, PLAIN)
            ) / (members - 1.0)
            for b in range(width // PIECE):
                at = slice(b * PIECE, (b + 1) * PIECE)
                spot = jnp.clip(first + b, 0, blocks_total - 1)
                top, low = split(gain[:, at] * cover_ref[spot, n].astype(jnp.float32))
                gain_top[place, at] = top
                gain_low[place, at] = low

    def increments(width, store):
        @pl.loop(0, members // TILE)
        def _(t):
            place = pl.ds(pl.multiple_of(t * TILE, TILE), TILE)
            left_top, left_low = weight_top[place, :], weight_low[place, :]
            right_top, right_low = gain_top[:, :width], gain_low[:, :width]
            store(
                place,
                dot(left_top, right_top, PLAIN)
                + dot(left_top, right_low, PLAIN)
                + dot(left_low, right_top, PLAIN),
            )

    def own_part(start, width):
        def store(place, value):
            result[place, start : start + width] = (
                states[place, edge + start : edge + start + width] + value
            )

        find_gain(edge + start, width)
        increments(width, store)

    def other_part(way):
        def store(place, value):
            edge_inc[way, place, :] = value

        find_gain((edge + own_width, 0)[way], edge)
        increments(edge, store)
        backward(way).start()

    def settle(way):
        start = (0, own_width - edge)[way]
        bound = offsets_ref[patch + way] - patch * per_device

        @pl.loop(0, members // TILE)
        def _(t):
            place = pl.ds(pl.multiple_of(t * TILE, TILE), TILE)
            for b in range(spread):
                block = start // PIECE + b
                foreign = at_least(bound, block + 1) if way == 0 else at_least(block, bound)
                at = slice(start + b * PIECE, start + (b + 1) * PIECE)
                theirs = (
                    states[place, edge + start + b * PIECE : edge + start + (b + 1) * PIECE]
                    + edge_got[way, place, b * PIECE : (b + 1) * PIECE]
                )
                result[place, at] = theirs * foreign + result[place, at] * (1.0 - foreign)

    take_states(S_MID, *pieces_of[S_MID])
    own_part(edge, middle)
    send_back(R_MID, edge, middle)
    take_states(S_HIGH, *pieces_of[S_HIGH])

    @pl.when(has_up)
    def _():
        forward(1).start()

    own_part(0, edge)

    @pl.when(has_up)
    def _():
        forward(0).wait_recv()
        other_part(0)

    own_part(own_width - edge, edge)

    @pl.when(has_dn)
    def _():
        forward(1).wait_recv()
        other_part(1)
        backward(0).wait_recv()
        settle(0)

    send_back(R_LOW, 0, edge)

    @pl.when(has_up)
    def _():
        backward(1).wait_recv()
        settle(1)

    send_back(R_HIGH, own_width - edge, edge)

    for copy in halo_copies:
        copy.wait_send()

    @pl.when(has_dn)
    def _():
        forward(0).wait_send()
        backward(1).wait_send()

    @pl.when(has_up)
    def _():
        forward(1).wait_send()
        backward(0).wait_send()

    for slot, (start, width) in pieces_of.items():

        @pl.loop(1, groups)
        def _(k):
            state_copy(slot, start, width, k).wait_send()

    @pl.loop(1, groups)
    def _(k):
        window_copy(W_D, pack.at[1], devs, k).wait_send()

    for slot, (start, width) in (
        (R_MID, pieces_of[S_MID]),
        (R_LOW, pieces_of[S_LOW]),
        (R_HIGH, pieces_of[S_HIGH]),
    ):

        @pl.loop(1, groups)
        def _(k):
            return_copy(slot, start, width, k).wait()

        return_own(slot, start, width).wait()


def body(
    row,
    background_realizations,
    realization_expected_data,
    departure_values,
    instrument_dispersion,
    window_piece_offsets,
    window_data_pieces,
    neighbor_piece_ids,
    coupling_indicator,
):
    groups = lax.axis_size("member")
    regions = lax.axis_size("region")
    rows, variable_total = background_realizations.shape
    obs_width = realization_expected_data.shape[1]
    members = groups * rows
    per_device = variable_total // PIECE // groups
    spread = (per_device - 1) // 2
    own_width = per_device * PIECE
    edge = spread * PIECE
    widest = max(edge, own_width - 2 * edge)
    side = neighbor_piece_ids.shape[-1]
    own_count = obs_width // PIECE
    ext_count = own_count + 2 * side
    f32, bf16 = jnp.float32, jnp.bfloat16
    smem = pl.BlockSpec(memory_space=pltpu.SMEM)
    hbm = pl.BlockSpec(memory_space=pl.ANY)
    return pl.pallas_call(
        functools.partial(analysis_kernel, (groups, regions, row, per_device, spread)),
        out_shape=jax.ShapeDtypeStruct((rows, variable_total), f32),
        in_specs=[smem, smem, smem, smem, hbm, hbm, hbm, pl.BlockSpec(memory_space=pltpu.VMEM)],
        out_specs=hbm,
        scratch_shapes=[
            pltpu.VMEM((rows, obs_width), f32),
            pltpu.VMEM((rows, obs_width), f32),
            pltpu.VMEM((own_count, rows, PIECE), f32),
            pltpu.VMEM((own_count, rows, PIECE), f32),
            pltpu.VMEM((ext_count, rows, PIECE), f32),
            pltpu.VMEM((ext_count, rows, PIECE), f32),
            pltpu.VMEM((ext_count, 1, PIECE), f32),
            pltpu.VMEM((2, 2, side, rows, PIECE), f32),
            pltpu.VMEM((2, side, 1, PIECE), f32),
            pltpu.VMEM((2, members, LOCAL), f32),
            pltpu.VMEM((members, LOCAL), f32),
            pltpu.VMEM((members, LOCAL), f32),
            pltpu.VMEM((members, own_width + 2 * edge), f32),
            pltpu.VMEM((LOCAL, members), f32),
            pltpu.VMEM((LOCAL, members), bf16),
            pltpu.VMEM((LOCAL, members), bf16),
            pltpu.VMEM((LOCAL, LOCAL), f32),
            pltpu.VMEM((PIECE, 2 * PIECE), f32),
            pltpu.VMEM((LOCAL, PIECE), f32),
            pltpu.VMEM((LOCAL, LOCAL), f32),
            pltpu.VMEM((members, LOCAL), bf16),
            pltpu.VMEM((members, LOCAL), bf16),
            pltpu.VMEM((LOCAL, widest), bf16),
            pltpu.VMEM((LOCAL, widest), bf16),
            pltpu.VMEM((members, widest), bf16),
            pltpu.VMEM((members, widest), bf16),
            pltpu.VMEM((members, own_width), f32),
            pltpu.VMEM((2, members, edge), f32),
            pltpu.VMEM((2, members, edge), f32),
            pltpu.SemaphoreType.DMA((8, groups)),
            pltpu.SemaphoreType.DMA((8, groups)),
            pltpu.SemaphoreType.DMA((4,)),
            pltpu.SemaphoreType.DMA((4,)),
            pltpu.SemaphoreType.DMA((3, 2)),
            pltpu.SemaphoreType.DMA((3, 2)),
            pltpu.SemaphoreType.DMA((2,)),
        ],
        compiler_params=pltpu.CompilerParams(
            collective_id=0, has_side_effects=True, vmem_limit_bytes=60 * 1024 * 1024
        ),
        name="analysis",
    )(
        window_data_pieces[0],
        neighbor_piece_ids[0],
        window_piece_offsets[0],
        coupling_indicator[0],
        background_realizations,
        realization_expected_data,
        departure_values,
        instrument_dispersion.reshape(-1, 1, PIECE),
    )


def row_length(mesh):
    devices = mesh.devices[:, 0].tolist()
    count = len(devices)
    spots = [getattr(d, "coords", None) for d in devices]
    if any(spot is None for spot in spots):
        return count
    row = 1
    while row < count and spots[row][2] == spots[0][2]:
        row += 1
    return row if count % row == 0 else count


def solution(mesh):
    return jax.shard_map(
        functools.partial(body, row_length(mesh)),
        mesh=mesh,
        in_specs=(
            P("member", "region"),
            P("member", "region"),
            P("member", "region"),
            P("region"),
            P("region", None),
            P("region", None, None),
            P("region", None, None),
            P("region", None, None),
        ),
        out_specs=P("member", "region"),
        check_vma=False,
    )
```

```python
import functools

import jax
import jax.numpy as jnp
from jax import lax
from jax.experimental import pallas as pl
from jax.experimental.pallas import tpu as pltpu
from jax.sharding import PartitionSpec as P

PIECE = 128
OBS_PER = 4
LOCAL = OBS_PER * PIECE
TILE = 256

MESH = pl.DeviceIdType.MESH
highest = lax.Precision.HIGHEST


def cols(start, count=1):
    return pl.ds(pl.multiple_of(start * PIECE, PIECE), count * PIECE)


def dot(left, right, contract, precision=None):
    return lax.dot_general(
        left,
        right,
        ((contract[0], contract[1]), ((), ())),
        precision=precision,
        preferred_element_type=jnp.float32,
    )


def at_least(value, bound):
    return jnp.clip(value - bound + 1, 0, 1).astype(jnp.float32)


PLAIN = ((1,), (0,))
BY_ROWS = ((1,), (1,))


def split(value):
    top = value.astype(jnp.bfloat16)
    return top, (value - top.astype(jnp.float32)).astype(jnp.bfloat16)


def factor_block(block, work_ref):
    size = block.shape[0]
    wide = 2 * size
    eye = lax.broadcasted_iota(jnp.int32, (size, size), 0) == lax.broadcasted_iota(
        jnp.int32, (size, size), 1
    )
    work_ref[:, :size] = block
    work_ref[:, size:] = eye.astype(jnp.float32)
    step_rows = 8
    row_ids = lax.broadcasted_iota(jnp.int32, (step_rows, wide), 0)
    for start in range(0, size, step_rows):
        rows = work_ref[start : start + step_rows, :]
        for j in range(step_rows):
            column = rows[:, start + j : start + j + 1]
            scale = 1.0 / jnp.sqrt(column[j : j + 1, :])
            pivot = rows[j : j + 1, :] * scale
            lowered = rows - (column * scale) * pivot
            rows = jnp.where(row_ids > j, lowered, jnp.where(row_ids == j, pivot, rows))
        work_ref[start : start + step_rows, :] = rows
        after = start + step_rows
        if after < size:
            change = dot(rows[:, :size], rows, ((0,), (0,)), highest)
            work_ref[after:, :] = work_ref[after:, :] - change[after:, :]


def snake(index, row, flip):
    return index + (index // row + flip) % 2 * (row - 1 - 2 * (index % row))


def analysis_kernel(
    plan,
    lists_ref,
    ids_ref,
    offsets_ref,
    cover_ref,
    background,
    expected_hbm,
    innov_hbm,
    flat_var,
    out,
    expected,
    innov,
    own_e,
    own_d,
    ext_e,
    ext_d,
    own_var,
    ext_var,
    halo_send,
    var_send,
    pack,
    obs,
    devs,
    states,
    turned,
    turned_top,
    turned_low,
    trailing,
    work,
    inverses,
    panels,
    weight_top,
    weight_low,
    gain_top,
    gain_low,
    state_top,
    state_low,
    result,
    edge_inc,
    edge_got,
    cross_got,
    member_send,
    member_recv,
    pair_send,
    pair_recv,
    halo_send_sem,
    halo_recv_sem,
    local_sem,
):
    groups, regions, row, per_device, spread = plan
    rows = expected.shape[0]
    own_count = expected.shape[1] // PIECE
    side = ids_ref.shape[2]
    members = groups * rows
    edge = spread * PIECE
    own_width = per_device * PIECE
    middle = own_width - 2 * edge
    me = lax.axis_index("member")
    region = lax.axis_index("region")
    flip = region % 2
    patch = snake(me, row, flip)
    has_dn = patch > 0
    has_up = patch < groups - 1
    near, far = groups // 2 - 1, groups // 2
    is_near, is_far = patch == near, patch == far
    gives_dn = jnp.logical_and(has_dn, patch != far)
    gives_up = jnp.logical_and(has_up, patch != near)
    owner_near = snake(near, row, flip)
    owner_far = snake(far, row, flip)
    lower = groups // 2
    in_lower = me < lower
    member_dn = snake((patch + groups - 1) % groups, row, flip)
    member_up = snake((patch + 1) % groups, row, flip)
    region_after = (region + 1) % regions
    region_before = (region + regions - 1) % regions
    my_rows = pl.ds(pl.multiple_of(me * rows, rows), rows)

    def rows_of(member):
        return pl.ds(pl.multiple_of(member * rows, rows), rows)

    load_e = pltpu.make_async_copy(expected_hbm, expected, local_sem.at[0])
    load_d = pltpu.make_async_copy(innov_hbm, innov, local_sem.at[1])
    load_e.start()
    load_d.start()

    barrier = pltpu.get_barrier_semaphore()
    for k in range(1, groups):
        pl.semaphore_signal(
            barrier, inc=1, device_id=((me + k) % groups, region), device_id_type=MESH
        )
    for other in (region_after, region_before):
        pl.semaphore_signal(barrier, inc=1, device_id=(me, other), device_id_type=MESH)
    pl.semaphore_wait(barrier, groups + 1)

    def state_copy(slot, start, width, k):
        target = (me + k) % groups
        source = snake(target, row, flip) * own_width + start
        return pltpu.make_async_remote_copy(
            src_ref=background.at[:, pl.ds(pl.multiple_of(source, PIECE), width)],
            dst_ref=states.at[my_rows, edge + start : edge + start + width],
            send_sem=member_send.at[slot, k],
            recv_sem=member_recv.at[slot, k],
            device_id=(target, region),
            device_id_type=MESH,
        )

    def state_own(slot, start, width):
        source = patch * own_width + start
        return pltpu.make_async_copy(
            background.at[:, pl.ds(pl.multiple_of(source, PIECE), width)],
            states.at[my_rows, edge + start : edge + start + width],
            member_recv.at[slot, 0],
        )

    def send_states(slot, start, width):
        @pl.loop(1, groups)
        def _(k):
            state_copy(slot, start, width, k).start()

        state_own(slot, start, width).start()

    def take_states(slot, start, width):
        @pl.loop(1, groups)
        def _(k):
            state_copy(slot, start, width, k).wait_recv()

        state_own(slot, start, width).wait()

    def middle_place(way):
        start = (near * own_width + own_width - edge, far * own_width)[way]
        landing = (0, edge + own_width)[way]
        return (
            background.at[:, start : start + edge],
            states.at[my_rows, landing : landing + edge],
        )

    def middle_copy(way, sender):
        source, target = middle_place(way)
        return pltpu.make_async_remote_copy(
            src_ref=source,
            dst_ref=target,
            send_sem=member_send.at[S_X, way],
            recv_sem=member_recv.at[S_X, sender],
            device_id=((owner_far, owner_near)[way], region),
            device_id_type=MESH,
        )

    def middle_own(way):
        return pltpu.make_async_copy(*middle_place(way), local_sem.at[2])

    def send_middle():
        for way, mine in ((0, is_far), (1, is_near)):

            @pl.when(jnp.logical_not(mine))
            def _():
                middle_copy(way, me).start()

            @pl.when(mine)
            def _():
                middle_own(way).start()

    def sent_middle():
        for way, mine in ((0, is_far), (1, is_near)):

            @pl.when(jnp.logical_not(mine))
            def _():
                middle_copy(way, me).wait_send()

    def take_middle(way):
        @pl.loop(1, groups)
        def _(k):
            middle_copy(way, (me + groups - k) % groups).wait_recv()

        middle_own(way).wait()

    def window_copy(slot, source, target_ref, k):
        return pltpu.make_async_remote_copy(
            src_ref=source.at[rows_of((me + k) % groups), :],
            dst_ref=target_ref.at[my_rows, :],
            send_sem=member_send.at[slot, k],
            recv_sem=member_recv.at[slot, k],
            device_id=((me + k) % groups, region),
            device_id_type=MESH,
        )

    def return_copy(slot, start, width, k):
        return pltpu.make_async_remote_copy(
            src_ref=result.at[rows_of((me + k) % groups), start : start + width],
            dst_ref=out.at[
                :, pl.ds(pl.multiple_of(patch * own_width + start, PIECE), width)
            ],
            send_sem=member_send.at[slot, k],
            recv_sem=member_recv.at[slot, k],
            device_id=((me + k) % groups, region),
            device_id_type=MESH,
        )

    def return_own(slot, start, width):
        return pltpu.make_async_copy(
            result.at[my_rows, start : start + width],
            out.at[:, pl.ds(pl.multiple_of(patch * own_width + start, PIECE), width)],
            member_recv.at[slot, 0],
        )

    def returns(slot, p, member):
        if slot == R_LOW:
            return jnp.logical_or(p != far, member >= lower)
        if slot == R_HIGH:
            return jnp.logical_or(p != near, member < lower)
        return p >= 0

    def send_back(slot, start, width):
        @pl.loop(1, groups)
        def _(k):
            @pl.when(returns(slot, patch, (me + k) % groups))
            def _():
                return_copy(slot, start, width, k).start()

        @pl.when(returns(slot, patch, me))
        def _():
            return_own(slot, start, width).start()

    def end_back(slot, start, width):
        @pl.loop(1, groups)
        def _(k):
            @pl.when(returns(slot, patch, (me + k) % groups))
            def _():
                return_copy(slot, start, width, k).wait_send()

            @pl.when(returns(slot, snake((me + groups - k) % groups, row, flip), me))
            def _():
                return_copy(slot, start, width, k).wait_recv()

        @pl.when(returns(slot, patch, me))
        def _():
            return_own(slot, start, width).wait()

    def cross_place(way, member):
        start = (far * own_width, near * own_width + own_width - edge)[way]
        return (
            edge_inc.at[way, rows_of(member), :],
            out.at[:, start : start + edge],
        )

    def cross_copy(way, member):
        source, target = cross_place(way, member)
        return pltpu.make_async_remote_copy(
            src_ref=source,
            dst_ref=target,
            send_sem=member_send.at[R_X, member],
            recv_sem=member_recv.at[R_X, 0],
            device_id=(member, region),
            device_id_type=MESH,
        )

    def cross_own(way):
        return pltpu.make_async_copy(*cross_place(way, me), local_sem.at[3])

    crossing = ((0, is_near, owner_near, 0, lower), (1, is_far, owner_far, lower, groups))

    def send_cross(way):
        first, last = crossing[way][3:]

        @pl.loop(first, last)
        def _(member):
            @pl.when(member != me)
            def _():
                cross_copy(way, member).start()

        @pl.when(jnp.logical_and(me >= first, me < last))
        def _():
            cross_own(way).start()

    def end_cross():
        for way, mine, owner, first, last in crossing:
            inside = jnp.logical_and(me >= first, me < last)

            @pl.when(mine)
            def _():
                @pl.loop(first, last)
                def _(member):
                    @pl.when(member != me)
                    def _():
                        cross_copy(way, member).wait_send()

                @pl.when(inside)
                def _():
                    cross_own(way).wait()

            @pl.when(jnp.logical_and(inside, me != owner))
            def _():
                cross_copy(way, me).wait_recv()

    S_MID, S_LOW, S_HIGH, W_E, W_D, R_MID, R_LOW, R_HIGH, S_X, R_X = range(10)
    pieces_of = {
        S_MID: (edge, middle),
        S_LOW: (0, edge),
        S_HIGH: (own_width - edge, edge),
    }

    send_states(S_MID, *pieces_of[S_MID])

    for load, flat, own, ext in (
        (load_e, expected, own_e, ext_e),
        (load_d, innov, own_d, ext_d),
    ):
        load.wait()
        for n in range(own_count):
            block = flat[:, n * PIECE : (n + 1) * PIECE]
            own[n] = block
            ext[n] = block
    for n in range(own_count):
        own_var[n] = flat_var[n : n + 1, :]
        ext_var[n] = flat_var[n : n + 1, :]
    halo_copies = []
    for part, (own, ext, send) in enumerate(
        ((own_e, ext_e, halo_send.at[0]), (own_var, ext_var, var_send), (own_d, ext_d, halo_send.at[1]))
    ):
        for way, other in ((0, region_after), (1, region_before)):
            for k in range(side):
                send[way, k] = own[ids_ref[0, way, k]]
            landing = own_count + way * side
            copy = pltpu.make_async_remote_copy(
                src_ref=send.at[way],
                dst_ref=ext.at[landing : landing + side],
                send_sem=halo_send_sem.at[part, way],
                recv_sem=halo_recv_sem.at[part, way],
                device_id=(me, other),
                device_id_type=MESH,
            )
            copy.start()
            halo_copies.append(copy)

    def pack_window(ext, buffer, k):
        target = (me + k) % groups
        p = snake(target, row, flip)
        for n in range(OBS_PER):
            buffer[rows_of(target), n * PIECE : (n + 1) * PIECE] = ext[lists_ref[0, p, n]]

    for copy in halo_copies[:2]:
        copy.wait_recv()

    @pl.loop(1, groups)
    def _(k):
        pack_window(ext_e, pack.at[0], k)
        window_copy(W_E, pack.at[0], obs, k).start()

    pack_window(ext_e, obs, 0)
    for copy in halo_copies[2:]:
        copy.wait_recv()
    variances = [ext_var[lists_ref[0, patch, n]] for n in range(OBS_PER)]

    @pl.loop(1, groups)
    def _(k):
        pack_window(ext_d, pack.at[1], k)

    pack_window(ext_d, devs, 0)

    @pl.loop(1, groups)
    def _(k):
        window_copy(W_E, pack.at[0], obs, k).wait_send()
        window_copy(W_D, pack.at[1], devs, k).start()

    @pl.loop(1, groups)
    def _(k):
        window_copy(W_E, pack.at[0], obs, k).wait_recv()

    tiles = members // PIECE

    def add_rows(t, total):
        part = obs[pl.ds(pl.multiple_of(t * PIECE, PIECE), PIECE), :]
        return total + jnp.sum(part, axis=0, keepdims=True)

    mean = lax.fori_loop(0, tiles, add_rows, jnp.zeros((1, LOCAL), jnp.float32)) / members

    @pl.loop(0, tiles)
    def _(t):
        place = pl.ds(pl.multiple_of(t * PIECE, PIECE), PIECE)
        part = obs[place, :] - mean
        obs[place, :] = part
        flat = part.T
        turned[:, place] = flat
        top, low = split(flat)
        turned_top[:, place] = top
        turned_low[:, place] = low

    @pl.loop(0, LOCAL // TILE)
    def _(i):
        place = pl.ds(pl.multiple_of(i * TILE, TILE), TILE)

        @pl.loop(0, LOCAL // TILE)
        def _(j):
            other = pl.ds(pl.multiple_of(j * TILE, TILE), TILE)
            trailing[place, other] = dot(
                turned[place, :], obs[:, other], PLAIN, highest
            ) / (members - 1.0)

    eye = lax.broadcasted_iota(jnp.int32, (PIECE, PIECE), 0) == lax.broadcasted_iota(
        jnp.int32, (PIECE, PIECE), 1
    )
    for n in range(OBS_PER):
        place = slice(n * PIECE, (n + 1) * PIECE)
        trailing[place, place] = trailing[place, place] + jnp.where(eye, variances[n], 0.0)

    line = lax.broadcasted_iota(jnp.int32, (LOCAL, PIECE), 0)

    @pl.loop(0, OBS_PER)
    def _(k):
        place = cols(k)
        factor_block(trailing[place, place], work)

        @pl.when(k == 0)
        def _():
            send_states(S_LOW, *pieces_of[S_LOW])

        @pl.when(k == 2)
        def _():
            send_middle()
            send_states(S_HIGH, *pieces_of[S_HIGH])

        inverse = work[:, PIECE:]
        inverses[place, :] = inverse
        panel = dot(trailing[:, place], inverse, BY_ROWS, highest)
        panel = jnp.where(line >= (k + 1) * PIECE, panel, 0.0)
        panels[:, place] = panel

        @pl.loop(0, LOCAL // PIECE)
        def _(i):
            part = cols(i)
            trailing[part, :] = trailing[part, :] - dot(
                panels[part, place], panels[:, place], BY_ROWS, highest
            )

    def forward(way):
        start, other = ((edge, member_dn), (own_width, member_up))[way]
        landing = (edge + own_width, 0)[way]
        return pltpu.make_async_remote_copy(
            src_ref=states.at[:, start : start + edge],
            dst_ref=states.at[:, landing : landing + edge],
            send_sem=pair_send.at[way],
            recv_sem=pair_recv.at[way],
            device_id=(other, region),
            device_id_type=MESH,
        )

    def backward(way):
        other = (member_up, member_dn)[way]
        return pltpu.make_async_remote_copy(
            src_ref=edge_inc.at[way],
            dst_ref=edge_got.at[way],
            send_sem=pair_send.at[2 + way],
            recv_sem=pair_recv.at[2 + way],
            device_id=(other, region),
            device_id_type=MESH,
        )

    take_states(S_LOW, *pieces_of[S_LOW])

    @pl.when(gives_dn)
    def _():
        forward(0).start()

    @pl.loop(1, groups)
    def _(k):
        window_copy(W_D, pack.at[1], devs, k).wait_recv()

    @pl.loop(0, members // TILE)
    def _(t):
        place = pl.ds(pl.multiple_of(t * TILE, TILE), TILE)
        rest = devs[place, :]
        parts = []
        for k in range(OBS_PER):
            at = slice(k * PIECE, (k + 1) * PIECE)
            part = dot(rest[:, :PIECE], inverses[at, :], BY_ROWS, highest)
            parts.append(part)
            if k + 1 < OBS_PER:
                rest = rest[:, PIECE:] - dot(
                    part, panels[(k + 1) * PIECE :, at], BY_ROWS, highest
                )
        done = None
        for k in reversed(range(OBS_PER)):
            at = slice(k * PIECE, (k + 1) * PIECE)
            part = parts[k]
            if done is not None:
                part = part - dot(done, panels[(k + 1) * PIECE :, at], PLAIN, highest)
            part = dot(part, inverses[at, :], PLAIN, highest)
            done = part if done is None else jnp.concatenate([part, done], axis=1)
        top, low = split(done)
        weight_top[place, :] = top
        weight_low[place, :] = low

    blocks_total = cover_ref.shape[1]

    def find_gain(start, width):
        def add_states(t, total):
            part = states[
                pl.ds(pl.multiple_of(t * PIECE, PIECE), PIECE), start : start + width
            ]
            return total + jnp.sum(part, axis=0, keepdims=True)

        centre = (
            lax.fori_loop(0, tiles, add_states, jnp.zeros((1, width), jnp.float32))
            / members
        )

        @pl.loop(0, tiles)
        def _(t):
            place = pl.ds(pl.multiple_of(t * PIECE, PIECE), PIECE)
            top, low = split(states[place, start : start + width] - centre)
            state_top[place, :width] = top
            state_low[place, :width] = low

        first = patch * per_device - spread + start // PIECE

        @pl.loop(0, OBS_PER)
        def _(n):
            place = cols(n)
            left_top, left_low = turned_top[place, :], turned_low[place, :]
            right_top, right_low = state_top[:, :width], state_low[:, :width]
            gain = (
                dot(left_top, right_top, PLAIN)
                + dot(left_top, right_low, PLAIN)
                + dot(left_low, right_top, PLAIN)
            ) / (members - 1.0)
            for b in range(width // PIECE):
                at = slice(b * PIECE, (b + 1) * PIECE)
                spot = jnp.clip(first + b, 0, blocks_total - 1)
                top, low = split(gain[:, at] * cover_ref[0, spot, n].astype(jnp.float32))
                gain_top[place, at] = top
                gain_low[place, at] = low

    def increments(width, store):
        @pl.loop(0, members // TILE)
        def _(t):
            place = pl.ds(pl.multiple_of(t * TILE, TILE), TILE)
            left_top, left_low = weight_top[place, :], weight_low[place, :]
            right_top, right_low = gain_top[:, :width], gain_low[:, :width]
            store(
                place,
                dot(left_top, right_top, PLAIN)
                + dot(left_top, right_low, PLAIN)
                + dot(left_low, right_top, PLAIN),
            )

    def own_part(start, width):
        def store(place, value):
            result[place, start : start + width] = (
                states[place, edge + start : edge + start + width] + value
            )

        find_gain(edge + start, width)
        increments(width, store)

    def other_part(way):
        place_in = (edge + own_width, 0)[way]

        def store(place, value):
            edge_inc[way, place, :] = states[place, place_in : place_in + edge] + value

        find_gain(place_in, edge)
        increments(edge, store)

    def foreign(way, owner, b):
        start = (0, own_width - edge)[way]
        bound = offsets_ref[0, owner + way] - owner * per_device
        block = start // PIECE + b
        return at_least(bound, block + 1) if way == 0 else at_least(block, bound)

    half_rows = lower * rows

    def settle(way, first=0, last=members):
        start = (0, own_width - edge)[way]

        @pl.loop(first // PIECE, last // PIECE)
        def _(t):
            place = pl.ds(pl.multiple_of(t * PIECE, PIECE), PIECE)
            for b in range(spread):
                share = foreign(way, patch, b)
                at = slice(start + b * PIECE, start + (b + 1) * PIECE)
                theirs = edge_got[way, place, b * PIECE : (b + 1) * PIECE]
                result[place, at] = theirs * share + result[place, at] * (1.0 - share)

    def settle_cross(way, owner, first, last):
        @pl.loop(first // PIECE, last // PIECE)
        def _(t):
            place = pl.ds(pl.multiple_of(t * PIECE, PIECE), PIECE)
            for b in range(spread):
                share = foreign(way, owner, b)
                at = slice(b * PIECE, (b + 1) * PIECE)
                mine = edge_inc[way, place, at]
                theirs = cross_got[place, at]
                edge_inc[way, place, at] = mine * share + theirs * (1.0 - share)

    def swap(near_sends, part):
        first = half_rows if near_sends else 0
        count = members - half_rows if near_sends else half_rows
        sent = slice(first, first + count)
        if part == 0:
            way = 0 if near_sends else 1
            source = edge_inc.at[way, sent, :]
            target = edge_got.at[way, sent, :]
        else:
            start = own_width - edge if near_sends else 0
            source = result.at[sent, start : start + edge]
            target = cross_got.at[sent, :]
        return pltpu.make_async_remote_copy(
            src_ref=source,
            dst_ref=target,
            send_sem=pair_send.at[4 + part],
            recv_sem=pair_recv.at[4 + part],
            device_id=(owner_far if near_sends else owner_near, region),
            device_id_type=MESH,
        )

    take_states(S_MID, *pieces_of[S_MID])
    own_part(edge, middle)
    send_back(R_MID, edge, middle)
    take_states(S_HIGH, *pieces_of[S_HIGH])

    @pl.when(gives_up)
    def _():
        forward(1).start()

    @pl.when(is_far)
    def _():
        take_middle(0)

    @pl.when(is_near)
    def _():
        take_middle(1)

    own_part(0, edge)

    @pl.when(is_far)
    def _():
        swap(False, 1).start()

    @pl.when(has_up)
    def _():
        @pl.when(gives_up)
        def _():
            forward(0).wait_recv()

        other_part(0)

        @pl.when(gives_up)
        def _():
            backward(0).start()

        @pl.when(is_near)
        def _():
            swap(True, 0).start()

    own_part(own_width - edge, edge)

    @pl.when(is_near)
    def _():
        swap(True, 1).start()

    @pl.when(has_dn)
    def _():
        @pl.when(gives_dn)
        def _():
            forward(1).wait_recv()

        other_part(1)

        @pl.when(gives_dn)
        def _():
            backward(1).start()
            backward(0).wait_recv()
            settle(0)

        @pl.when(is_far)
        def _():
            swap(False, 0).start()
            swap(True, 0).wait_recv()
            settle(0, half_rows, members)

    send_back(R_LOW, 0, edge)

    @pl.when(gives_up)
    def _():
        backward(1).wait_recv()
        settle(1)

    @pl.when(is_near)
    def _():
        swap(False, 0).wait_recv()
        settle(1, 0, half_rows)

    send_back(R_HIGH, own_width - edge, edge)

    @pl.when(is_near)
    def _():
        swap(True, 0).wait_send()
        swap(False, 1).wait_recv()
        settle_cross(0, far, 0, half_rows)
        send_cross(0)

    @pl.when(is_far)
    def _():
        swap(False, 0).wait_send()
        swap(True, 1).wait_recv()
        settle_cross(1, near, half_rows, members)
        send_cross(1)

    for copy in halo_copies:
        copy.wait_send()

    @pl.when(gives_dn)
    def _():
        forward(0).wait_send()
        backward(1).wait_send()

    @pl.when(gives_up)
    def _():
        forward(1).wait_send()
        backward(0).wait_send()

    @pl.when(is_near)
    def _():
        swap(True, 1).wait_send()

    @pl.when(is_far)
    def _():
        swap(False, 1).wait_send()

    sent_middle()
    end_cross()

    for slot, (start, width) in pieces_of.items():

        @pl.loop(1, groups)
        def _(k):
            state_copy(slot, start, width, k).wait_send()

    @pl.loop(1, groups)
    def _(k):
        window_copy(W_D, pack.at[1], devs, k).wait_send()

    for slot, (start, width) in (
        (R_MID, pieces_of[S_MID]),
        (R_LOW, pieces_of[S_LOW]),
        (R_HIGH, pieces_of[S_HIGH]),
    ):
        end_back(slot, start, width)


def body(
    row,
    background_realizations,
    realization_expected_data,
    departure_values,
    instrument_dispersion,
    window_piece_offsets,
    window_data_pieces,
    neighbor_piece_ids,
    coupling_indicator,
):
    groups = lax.axis_size("member")
    regions = lax.axis_size("region")
    rows, variable_total = background_realizations.shape
    obs_width = realization_expected_data.shape[1]
    members = groups * rows
    per_device = variable_total // PIECE // groups
    spread = (per_device - 1) // 2
    own_width = per_device * PIECE
    edge = spread * PIECE
    widest = max(edge, own_width - 2 * edge)
    side = neighbor_piece_ids.shape[-1]
    own_count = obs_width // PIECE
    ext_count = own_count + 2 * side
    f32, bf16 = jnp.float32, jnp.bfloat16
    smem = pl.BlockSpec(memory_space=pltpu.SMEM)
    hbm = pl.BlockSpec(memory_space=pl.ANY)
    return pl.pallas_call(
        functools.partial(analysis_kernel, (groups, regions, row, per_device, spread)),
        out_shape=jax.ShapeDtypeStruct((rows, variable_total), f32),
        in_specs=[smem, smem, smem, smem, hbm, hbm, hbm, pl.BlockSpec(memory_space=pltpu.VMEM)],
        out_specs=hbm,
        scratch_shapes=[
            pltpu.VMEM((rows, obs_width), f32),
            pltpu.VMEM((rows, obs_width), f32),
            pltpu.VMEM((own_count, rows, PIECE), f32),
            pltpu.VMEM((own_count, rows, PIECE), f32),
            pltpu.VMEM((ext_count, rows, PIECE), f32),
            pltpu.VMEM((ext_count, rows, PIECE), f32),
            pltpu.VMEM((own_count, 1, PIECE), f32),
            pltpu.VMEM((ext_count, 1, PIECE), f32),
            pltpu.VMEM((2, 2, side, rows, PIECE), f32),
            pltpu.VMEM((2, side, 1, PIECE), f32),
            pltpu.VMEM((2, members, LOCAL), f32),
            pltpu.VMEM((members, LOCAL), f32),
            pltpu.VMEM((members, LOCAL), f32),
            pltpu.VMEM((members, own_width + 2 * edge), f32),
            pltpu.VMEM((LOCAL, members), f32),
            pltpu.VMEM((LOCAL, members), bf16),
            pltpu.VMEM((LOCAL, members), bf16),
            pltpu.VMEM((LOCAL, LOCAL), f32),
            pltpu.VMEM((PIECE, 2 * PIECE), f32),
            pltpu.VMEM((LOCAL, PIECE), f32),
            pltpu.VMEM((LOCAL, LOCAL), f32),
            pltpu.VMEM((members, LOCAL), bf16),
            pltpu.VMEM((members, LOCAL), bf16),
            pltpu.VMEM((LOCAL, widest), bf16),
            pltpu.VMEM((LOCAL, widest), bf16),
            pltpu.VMEM((members, widest), bf16),
            pltpu.VMEM((members, widest), bf16),
            pltpu.VMEM((members, own_width), f32),
            pltpu.VMEM((2, members, edge), f32),
            pltpu.VMEM((2, members, edge), f32),
            pltpu.VMEM((members, edge), f32),
            pltpu.SemaphoreType.DMA((10, groups)),
            pltpu.SemaphoreType.DMA((10, groups)),
            pltpu.SemaphoreType.DMA((6,)),
            pltpu.SemaphoreType.DMA((6,)),
            pltpu.SemaphoreType.DMA((3, 2)),
            pltpu.SemaphoreType.DMA((3, 2)),
            pltpu.SemaphoreType.DMA((4,)),
        ],
        compiler_params=pltpu.CompilerParams(
            collective_id=0, has_side_effects=True, vmem_limit_bytes=60 * 1024 * 1024
        ),
        name="analysis",
    )(
        window_data_pieces,
        neighbor_piece_ids,
        window_piece_offsets,
        coupling_indicator,
        background_realizations,
        realization_expected_data,
        departure_values,
        instrument_dispersion.reshape(-1, PIECE),
    )


def row_length(mesh):
    devices = mesh.devices[:, 0].tolist()
    count = len(devices)
    spots = [getattr(d, "coords", None) for d in devices]
    if any(spot is None for spot in spots):
        return count
    row = 1
    while row < count and spots[row][2] == spots[0][2]:
        row += 1
    return row if count % row == 0 else count


def solution(mesh):
    return jax.shard_map(
        functools.partial(body, row_length(mesh)),
        mesh=mesh,
        in_specs=(
            P("member", "region"),
            P("member", "region"),
            P("member", "region"),
            P("region"),
            P("region", None),
            P("region", None, None),
            P("region", None, None),
            P("region", None, None),
        ),
        out_specs=P("member", "region"),
        check_vma=False,
    )
```

```python
import functools

import jax
import jax.numpy as jnp
from jax import lax
from jax.experimental import pallas as pl
from jax.experimental.pallas import tpu as pltpu
from jax.sharding import PartitionSpec as P

PIECE = 128
OBS_PER = 4
LOCAL = OBS_PER * PIECE
TILE = 256

MESH = pl.DeviceIdType.MESH
highest = lax.Precision.HIGHEST


def cols(start, count=1):
    return pl.ds(pl.multiple_of(start * PIECE, PIECE), count * PIECE)


def dot(left, right, contract, precision=None):
    return lax.dot_general(
        left,
        right,
        ((contract[0], contract[1]), ((), ())),
        precision=precision,
        preferred_element_type=jnp.float32,
    )


def at_least(value, bound):
    return jnp.clip(value - bound + 1, 0, 1).astype(jnp.float32)


PLAIN = ((1,), (0,))
BY_ROWS = ((1,), (1,))


def split(value):
    top = value.astype(jnp.bfloat16)
    return top, (value - top.astype(jnp.float32)).astype(jnp.bfloat16)


def factor_block(block, work_ref):
    size = block.shape[0]
    wide = 2 * size
    eye = lax.broadcasted_iota(jnp.int32, (size, size), 0) == lax.broadcasted_iota(
        jnp.int32, (size, size), 1
    )
    work_ref[:, :size] = block
    work_ref[:, size:] = eye.astype(jnp.float32)
    step_rows = 8
    row_ids = lax.broadcasted_iota(jnp.int32, (step_rows, wide), 0)
    for start in range(0, size, step_rows):
        rows = work_ref[start : start + step_rows, :]
        for j in range(step_rows):
            column = rows[:, start + j : start + j + 1]
            scale = 1.0 / jnp.sqrt(column[j : j + 1, :])
            pivot = rows[j : j + 1, :] * scale
            lowered = rows - (column * scale) * pivot
            rows = jnp.where(row_ids > j, lowered, jnp.where(row_ids == j, pivot, rows))
        work_ref[start : start + step_rows, :] = rows
        after = start + step_rows
        if after < size:
            change = dot(rows[:, :size], rows, ((0,), (0,)), highest)
            work_ref[after:, :] = work_ref[after:, :] - change[after:, :]


def snake(index, row, flip):
    return index + (index // row + flip) % 2 * (row - 1 - 2 * (index % row))


def analysis_kernel(
    plan,
    lists_ref,
    ids_ref,
    offsets_ref,
    cover_ref,
    background,
    expected_hbm,
    innov_hbm,
    flat_var,
    out,
    expected,
    innov,
    own_e,
    own_d,
    ext_e,
    ext_d,
    own_var,
    ext_var,
    halo_send,
    var_send,
    pack,
    obs,
    devs,
    states,
    turned,
    turned_top,
    turned_low,
    trailing,
    work,
    inverses,
    panels,
    weight_top,
    weight_low,
    gain_top,
    gain_low,
    state_top,
    state_low,
    result,
    edge_inc,
    edge_got,
    cross_got,
    member_send,
    member_recv,
    pair_send,
    pair_recv,
    halo_send_sem,
    halo_recv_sem,
    local_sem,
):
    groups, regions, row, per_device, spread = plan
    rows = expected.shape[0]
    own_count = expected.shape[1] // PIECE
    side = ids_ref.shape[2]
    members = groups * rows
    edge = spread * PIECE
    own_width = per_device * PIECE
    middle = own_width - 2 * edge
    me = lax.axis_index("member")
    region = lax.axis_index("region")
    flip = region % 2
    patch = snake(me, row, flip)
    has_dn = patch > 0
    has_up = patch < groups - 1
    near, far = groups // 2 - 1, groups // 2
    is_near, is_far = patch == near, patch == far
    gives_dn = jnp.logical_and(has_dn, patch != far)
    gives_up = jnp.logical_and(has_up, patch != near)
    owner_near = snake(near, row, flip)
    owner_far = snake(far, row, flip)
    lower = groups // 2
    in_lower = me < lower
    member_dn = snake((patch + groups - 1) % groups, row, flip)
    member_up = snake((patch + 1) % groups, row, flip)
    region_after = (region + 1) % regions
    region_before = (region + regions - 1) % regions
    my_rows = pl.ds(pl.multiple_of(me * rows, rows), rows)

    def rows_of(member):
        return pl.ds(pl.multiple_of(member * rows, rows), rows)

    load_e = pltpu.make_async_copy(expected_hbm, expected, local_sem.at[0])
    load_d = pltpu.make_async_copy(innov_hbm, innov, local_sem.at[1])
    load_e.start()
    load_d.start()

    barrier = pltpu.get_barrier_semaphore()
    for k in range(1, groups):
        pl.semaphore_signal(
            barrier, inc=1, device_id=((me + k) % groups, region), device_id_type=MESH
        )
    for other in (region_after, region_before):
        pl.semaphore_signal(barrier, inc=1, device_id=(me, other), device_id_type=MESH)
    pl.semaphore_wait(barrier, groups + 1)

    def state_copy(slot, start, width, k):
        target = (me + k) % groups
        source = snake(target, row, flip) * own_width + start
        return pltpu.make_async_remote_copy(
            src_ref=background.at[:, pl.ds(pl.multiple_of(source, PIECE), width)],
            dst_ref=states.at[my_rows, edge + start : edge + start + width],
            send_sem=member_send.at[slot, k],
            recv_sem=member_recv.at[slot, k],
            device_id=(target, region),
            device_id_type=MESH,
        )

    def state_own(slot, start, width):
        source = patch * own_width + start
        return pltpu.make_async_copy(
            background.at[:, pl.ds(pl.multiple_of(source, PIECE), width)],
            states.at[my_rows, edge + start : edge + start + width],
            member_recv.at[slot, 0],
        )

    def send_states(slot, start, width):
        @pl.loop(1, groups)
        def _(k):
            state_copy(slot, start, width, k).start()

        state_own(slot, start, width).start()

    def take_states(slot, start, width):
        @pl.loop(1, groups)
        def _(k):
            state_copy(slot, start, width, k).wait_recv()

        state_own(slot, start, width).wait()

    def middle_place(way):
        start = (near * own_width + own_width - edge, far * own_width)[way]
        landing = (0, edge + own_width)[way]
        return (
            background.at[:, start : start + edge],
            states.at[my_rows, landing : landing + edge],
        )

    def middle_copy(way, sender):
        source, target = middle_place(way)
        return pltpu.make_async_remote_copy(
            src_ref=source,
            dst_ref=target,
            send_sem=member_send.at[S_X, way],
            recv_sem=member_recv.at[S_X, sender],
            device_id=((owner_far, owner_near)[way], region),
            device_id_type=MESH,
        )

    def middle_own(way):
        return pltpu.make_async_copy(*middle_place(way), local_sem.at[2])

    def send_middle():
        for way, mine in ((0, is_far), (1, is_near)):

            @pl.when(jnp.logical_not(mine))
            def _():
                middle_copy(way, me).start()

            @pl.when(mine)
            def _():
                middle_own(way).start()

    def sent_middle():
        for way, mine in ((0, is_far), (1, is_near)):

            @pl.when(jnp.logical_not(mine))
            def _():
                middle_copy(way, me).wait_send()

    def take_middle(way):
        @pl.loop(1, groups)
        def _(k):
            middle_copy(way, (me + groups - k) % groups).wait_recv()

        middle_own(way).wait()

    def window_copy(slot, source, target_ref, k):
        return pltpu.make_async_remote_copy(
            src_ref=source.at[rows_of((me + k) % groups), :],
            dst_ref=target_ref.at[my_rows, :],
            send_sem=member_send.at[slot, k],
            recv_sem=member_recv.at[slot, k],
            device_id=((me + k) % groups, region),
            device_id_type=MESH,
        )

    def return_copy(slot, start, width, k):
        return pltpu.make_async_remote_copy(
            src_ref=result.at[rows_of((me + k) % groups), start : start + width],
            dst_ref=out.at[
                :, pl.ds(pl.multiple_of(patch * own_width + start, PIECE), width)
            ],
            send_sem=member_send.at[slot, k],
            recv_sem=member_recv.at[slot, k],
            device_id=((me + k) % groups, region),
            device_id_type=MESH,
        )

    def return_own(slot, start, width):
        return pltpu.make_async_copy(
            result.at[my_rows, start : start + width],
            out.at[:, pl.ds(pl.multiple_of(patch * own_width + start, PIECE), width)],
            member_recv.at[slot, 0],
        )

    def returns(slot, p, member):
        if slot == R_LOW:
            return jnp.logical_or(p != far, member >= lower)
        if slot == R_HIGH:
            return jnp.logical_or(p != near, member < lower)
        return p >= 0

    def send_back(slot, start, width):
        @pl.loop(1, groups)
        def _(k):
            @pl.when(returns(slot, patch, (me + k) % groups))
            def _():
                return_copy(slot, start, width, k).start()

        @pl.when(returns(slot, patch, me))
        def _():
            return_own(slot, start, width).start()

    def end_back(slot, start, width):
        @pl.loop(1, groups)
        def _(k):
            @pl.when(returns(slot, patch, (me + k) % groups))
            def _():
                return_copy(slot, start, width, k).wait_send()

            @pl.when(returns(slot, snake((me + groups - k) % groups, row, flip), me))
            def _():
                return_copy(slot, start, width, k).wait_recv()

        @pl.when(returns(slot, patch, me))
        def _():
            return_own(slot, start, width).wait()

    def cross_place(way, member):
        start = (far * own_width, near * own_width + own_width - edge)[way]
        return (
            edge_inc.at[way, rows_of(member), :],
            out.at[:, start : start + edge],
        )

    def cross_copy(way, member):
        source, target = cross_place(way, member)
        return pltpu.make_async_remote_copy(
            src_ref=source,
            dst_ref=target,
            send_sem=member_send.at[R_X, member],
            recv_sem=member_recv.at[R_X, 0],
            device_id=(member, region),
            device_id_type=MESH,
        )

    def cross_own(way):
        return pltpu.make_async_copy(*cross_place(way, me), local_sem.at[3])

    crossing = ((0, is_near, owner_near, 0, lower), (1, is_far, owner_far, lower, groups))

    def send_cross(way):
        first, last = crossing[way][3:]

        @pl.loop(first, last)
        def _(member):
            @pl.when(member != me)
            def _():
                cross_copy(way, member).start()

        @pl.when(jnp.logical_and(me >= first, me < last))
        def _():
            cross_own(way).start()

    def end_cross():
        for way, mine, owner, first, last in crossing:
            inside = jnp.logical_and(me >= first, me < last)

            @pl.when(mine)
            def _():
                @pl.loop(first, last)
                def _(member):
                    @pl.when(member != me)
                    def _():
                        cross_copy(way, member).wait_send()

                @pl.when(inside)
                def _():
                    cross_own(way).wait()

            @pl.when(jnp.logical_and(inside, me != owner))
            def _():
                cross_copy(way, me).wait_recv()

    S_MID, S_NEXT, S_LOW, S_HIGH, W_E, W_D, R_MID, R_LOW, R_HIGH, S_X, R_X = range(11)
    pieces_of = {
        S_MID: (edge, PIECE),
        S_NEXT: (edge + PIECE, middle - PIECE),
        S_LOW: (0, edge),
        S_HIGH: (own_width - edge, edge),
    }

    send_states(S_MID, *pieces_of[S_MID])

    for load, flat, own, ext in (
        (load_e, expected, own_e, ext_e),
        (load_d, innov, own_d, ext_d),
    ):
        load.wait()
        for n in range(own_count):
            block = flat[:, n * PIECE : (n + 1) * PIECE]
            own[n] = block
            ext[n] = block
    for n in range(own_count):
        own_var[n] = flat_var[n : n + 1, :]
        ext_var[n] = flat_var[n : n + 1, :]
    halo_copies = []
    for part, (own, ext, send) in enumerate(
        ((own_e, ext_e, halo_send.at[0]), (own_var, ext_var, var_send), (own_d, ext_d, halo_send.at[1]))
    ):
        for way, other in ((0, region_after), (1, region_before)):
            for k in range(side):
                send[way, k] = own[ids_ref[0, way, k]]
            landing = own_count + way * side
            copy = pltpu.make_async_remote_copy(
                src_ref=send.at[way],
                dst_ref=ext.at[landing : landing + side],
                send_sem=halo_send_sem.at[part, way],
                recv_sem=halo_recv_sem.at[part, way],
                device_id=(me, other),
                device_id_type=MESH,
            )
            copy.start()
            halo_copies.append(copy)

    def pack_window(ext, buffer, k):
        target = (me + k) % groups
        p = snake(target, row, flip)
        for n in range(OBS_PER):
            buffer[rows_of(target), n * PIECE : (n + 1) * PIECE] = ext[lists_ref[0, n, p]]

    for copy in halo_copies[:2]:
        copy.wait_recv()

    @pl.loop(1, groups)
    def _(k):
        pack_window(ext_e, pack.at[0], k)
        window_copy(W_E, pack.at[0], obs, k).start()

    pack_window(ext_e, obs, 0)
    for copy in halo_copies[2:]:
        copy.wait_recv()
    variances = [ext_var[lists_ref[0, n, patch]] for n in range(OBS_PER)]

    @pl.loop(1, groups)
    def _(k):
        pack_window(ext_d, pack.at[1], k)

    pack_window(ext_d, devs, 0)

    @pl.loop(1, groups)
    def _(k):
        window_copy(W_E, pack.at[0], obs, k).wait_send()

    send_states(S_LOW, *pieces_of[S_LOW])
    send_middle()
    send_states(S_HIGH, *pieces_of[S_HIGH])

    @pl.loop(1, groups)
    def _(k):
        window_copy(W_E, pack.at[0], obs, k).wait_recv()

    tiles = members // PIECE

    def add_rows(t, total):
        part = obs[pl.ds(pl.multiple_of(t * PIECE, PIECE), PIECE), :]
        return total + jnp.sum(part, axis=0, keepdims=True)

    mean = lax.fori_loop(0, tiles, add_rows, jnp.zeros((1, LOCAL), jnp.float32)) / members

    @pl.loop(0, tiles)
    def _(t):
        place = pl.ds(pl.multiple_of(t * PIECE, PIECE), PIECE)
        part = obs[place, :] - mean
        obs[place, :] = part
        flat = part.T
        turned[:, place] = flat
        top, low = split(flat)
        turned_top[:, place] = top
        turned_low[:, place] = low

    @pl.loop(0, LOCAL // TILE)
    def _(i):
        place = pl.ds(pl.multiple_of(i * TILE, TILE), TILE)

        @pl.loop(0, LOCAL // TILE)
        def _(j):
            other = pl.ds(pl.multiple_of(j * TILE, TILE), TILE)
            trailing[place, other] = dot(
                turned[place, :], obs[:, other], PLAIN, highest
            ) / (members - 1.0)

    eye = lax.broadcasted_iota(jnp.int32, (PIECE, PIECE), 0) == lax.broadcasted_iota(
        jnp.int32, (PIECE, PIECE), 1
    )
    for n in range(OBS_PER):
        place = slice(n * PIECE, (n + 1) * PIECE)
        trailing[place, place] = trailing[place, place] + jnp.where(eye, variances[n], 0.0)

    def forward(way):
        start, other = ((edge, member_dn), (own_width, member_up))[way]
        landing = (edge + own_width, 0)[way]
        return pltpu.make_async_remote_copy(
            src_ref=states.at[:, start : start + edge],
            dst_ref=states.at[:, landing : landing + edge],
            send_sem=pair_send.at[way],
            recv_sem=pair_recv.at[way],
            device_id=(other, region),
            device_id_type=MESH,
        )

    def backward(way):
        other = (member_up, member_dn)[way]
        return pltpu.make_async_remote_copy(
            src_ref=edge_inc.at[way],
            dst_ref=edge_got.at[way],
            send_sem=pair_send.at[2 + way],
            recv_sem=pair_recv.at[2 + way],
            device_id=(other, region),
            device_id_type=MESH,
        )

    line = lax.broadcasted_iota(jnp.int32, (LOCAL, PIECE), 0)

    @pl.loop(0, OBS_PER)
    def _(k):
        place = cols(k)
        @pl.when(k == 2)
        def _():
            @pl.loop(1, groups)
            def _(j):
                window_copy(W_D, pack.at[1], devs, j).start()

            send_states(S_NEXT, *pieces_of[S_NEXT])

        @pl.when(k == 3)
        def _():
            take_states(S_LOW, *pieces_of[S_LOW])

            @pl.when(gives_dn)
            def _():
                forward(0).start()

            take_states(S_HIGH, *pieces_of[S_HIGH])

            @pl.when(gives_up)
            def _():
                forward(1).start()

        factor_block(trailing[place, place], work)

        inverse = work[:, PIECE:]
        inverses[place, :] = inverse
        panel = dot(trailing[:, place], inverse, BY_ROWS, highest)
        panel = jnp.where(line >= (k + 1) * PIECE, panel, 0.0)
        panels[:, place] = panel

        @pl.loop(0, LOCAL // PIECE)
        def _(i):
            part = cols(i)
            trailing[part, :] = trailing[part, :] - dot(
                panels[part, place], panels[:, place], BY_ROWS, highest
            )

    blocks_total = cover_ref.shape[2]

    def find_gain(start, width):
        def add_states(t, total):
            part = states[
                pl.ds(pl.multiple_of(t * PIECE, PIECE), PIECE), start : start + width
            ]
            return total + jnp.sum(part, axis=0, keepdims=True)

        centre = (
            lax.fori_loop(0, tiles, add_states, jnp.zeros((1, width), jnp.float32))
            / members
        )

        @pl.loop(0, tiles)
        def _(t):
            place = pl.ds(pl.multiple_of(t * PIECE, PIECE), PIECE)
            top, low = split(states[place, start : start + width] - centre)
            state_top[place, :width] = top
            state_low[place, :width] = low

        first = patch * per_device - spread + start // PIECE

        @pl.loop(0, OBS_PER)
        def _(n):
            place = cols(n)
            left_top, left_low = turned_top[place, :], turned_low[place, :]
            right_top, right_low = state_top[:, :width], state_low[:, :width]
            gain = (
                dot(left_top, right_top, PLAIN)
                + dot(left_top, right_low, PLAIN)
                + dot(left_low, right_top, PLAIN)
            ) / (members - 1.0)
            for b in range(width // PIECE):
                at = slice(b * PIECE, (b + 1) * PIECE)
                spot = jnp.clip(first + b, 0, blocks_total - 1)
                top, low = split(gain[:, at] * cover_ref[0, n, spot].astype(jnp.float32))
                gain_top[place, start + b * PIECE : start + (b + 1) * PIECE] = top
                gain_low[place, start + b * PIECE : start + (b + 1) * PIECE] = low

    find_gain(edge, edge)
    find_gain(own_width, edge)

    @pl.loop(1, groups)
    def _(k):
        window_copy(W_D, pack.at[1], devs, k).wait_recv()

    @pl.loop(0, members // TILE)
    def _(t):
        place = pl.ds(pl.multiple_of(t * TILE, TILE), TILE)
        rest = devs[place, :]
        parts = []
        for k in range(OBS_PER):
            at = slice(k * PIECE, (k + 1) * PIECE)
            part = dot(rest[:, :PIECE], inverses[at, :], BY_ROWS, highest)
            parts.append(part)
            if k + 1 < OBS_PER:
                rest = rest[:, PIECE:] - dot(
                    part, panels[(k + 1) * PIECE :, at], BY_ROWS, highest
                )
        done = None
        for k in reversed(range(OBS_PER)):
            at = slice(k * PIECE, (k + 1) * PIECE)
            part = parts[k]
            if done is not None:
                part = part - dot(done, panels[(k + 1) * PIECE :, at], PLAIN, highest)
            part = dot(part, inverses[at, :], PLAIN, highest)
            done = part if done is None else jnp.concatenate([part, done], axis=1)
        top, low = split(done)
        weight_top[place, :] = top
        weight_low[place, :] = low

    def increments(start, width, store):
        @pl.loop(0, members // TILE)
        def _(t):
            place = pl.ds(pl.multiple_of(t * TILE, TILE), TILE)
            left_top, left_low = weight_top[place, :], weight_low[place, :]
            right_top = gain_top[:, start : start + width]
            right_low = gain_low[:, start : start + width]
            store(
                place,
                dot(left_top, right_top, PLAIN)
                + dot(left_top, right_low, PLAIN)
                + dot(left_low, right_top, PLAIN),
            )

    def own_part(start, width):
        def store(place, value):
            result[place, start : start + width] = (
                states[place, edge + start : edge + start + width] + value
            )

        increments(edge + start, width, store)

    def other_part(way):
        place_in = (edge + own_width, 0)[way]

        def store(place, value):
            edge_inc[way, place, :] = states[place, place_in : place_in + edge] + value

        find_gain(place_in, edge)
        increments(place_in, edge, store)

    def foreign(way, owner, b):
        start = (0, own_width - edge)[way]
        bound = offsets_ref[0, owner + way] - owner * per_device
        block = start // PIECE + b
        return at_least(bound, block + 1) if way == 0 else at_least(block, bound)

    half_rows = lower * rows

    def settle(way, first=0, last=members):
        start = (0, own_width - edge)[way]

        @pl.loop(first // PIECE, last // PIECE)
        def _(t):
            place = pl.ds(pl.multiple_of(t * PIECE, PIECE), PIECE)
            for b in range(spread):
                share = foreign(way, patch, b)
                at = slice(start + b * PIECE, start + (b + 1) * PIECE)
                theirs = edge_got[way, place, b * PIECE : (b + 1) * PIECE]
                result[place, at] = theirs * share + result[place, at] * (1.0 - share)

    def settle_cross(way, owner, first, last):
        @pl.loop(first // PIECE, last // PIECE)
        def _(t):
            place = pl.ds(pl.multiple_of(t * PIECE, PIECE), PIECE)
            for b in range(spread):
                share = foreign(way, owner, b)
                at = slice(b * PIECE, (b + 1) * PIECE)
                mine = edge_inc[way, place, at]
                theirs = cross_got[place, at]
                edge_inc[way, place, at] = mine * share + theirs * (1.0 - share)

    def swap(near_sends, part):
        first = half_rows if near_sends else 0
        count = members - half_rows if near_sends else half_rows
        sent = slice(first, first + count)
        if part == 0:
            way = 0 if near_sends else 1
            source = edge_inc.at[way, sent, :]
            target = edge_got.at[way, sent, :]
        else:
            start = own_width - edge if near_sends else 0
            source = result.at[sent, start : start + edge]
            target = cross_got.at[sent, :]
        return pltpu.make_async_remote_copy(
            src_ref=source,
            dst_ref=target,
            send_sem=pair_send.at[4 + part],
            recv_sem=pair_recv.at[4 + part],
            device_id=(owner_far if near_sends else owner_near, region),
            device_id_type=MESH,
        )

    @pl.when(has_up)
    def _():
        @pl.when(gives_up)
        def _():
            forward(0).wait_recv()

        @pl.when(is_near)
        def _():
            take_middle(1)

        other_part(0)

        @pl.when(gives_up)
        def _():
            backward(0).start()

        @pl.when(is_near)
        def _():
            swap(True, 0).start()

    @pl.when(has_dn)
    def _():
        @pl.when(gives_dn)
        def _():
            forward(1).wait_recv()

        @pl.when(is_far)
        def _():
            take_middle(0)

        other_part(1)

        @pl.when(gives_dn)
        def _():
            backward(1).start()

        @pl.when(is_far)
        def _():
            swap(False, 0).start()

    take_states(S_MID, *pieces_of[S_MID])
    take_states(S_NEXT, *pieces_of[S_NEXT])
    find_gain(edge + edge, middle)
    own_part(edge, middle)
    send_back(R_MID, edge, middle)
    own_part(0, edge)

    @pl.when(is_far)
    def _():
        swap(False, 1).start()

    own_part(own_width - edge, edge)

    @pl.when(is_near)
    def _():
        swap(True, 1).start()

    @pl.when(gives_dn)
    def _():
        backward(0).wait_recv()
        settle(0)

    @pl.when(is_far)
    def _():
        swap(True, 0).wait_recv()
        settle(0, half_rows, members)

    send_back(R_LOW, 0, edge)

    @pl.when(gives_up)
    def _():
        backward(1).wait_recv()
        settle(1)

    @pl.when(is_near)
    def _():
        swap(False, 0).wait_recv()
        settle(1, 0, half_rows)

    send_back(R_HIGH, own_width - edge, edge)

    @pl.when(is_near)
    def _():
        swap(True, 0).wait_send()
        swap(False, 1).wait_recv()
        settle_cross(0, far, 0, half_rows)
        send_cross(0)

    @pl.when(is_far)
    def _():
        swap(False, 0).wait_send()
        swap(True, 1).wait_recv()
        settle_cross(1, near, half_rows, members)
        send_cross(1)

    for copy in halo_copies:
        copy.wait_send()

    @pl.when(gives_dn)
    def _():
        forward(0).wait_send()
        backward(1).wait_send()

    @pl.when(gives_up)
    def _():
        forward(1).wait_send()
        backward(0).wait_send()

    @pl.when(is_near)
    def _():
        swap(True, 1).wait_send()

    @pl.when(is_far)
    def _():
        swap(False, 1).wait_send()

    sent_middle()
    end_cross()

    for slot, (start, width) in pieces_of.items():

        @pl.loop(1, groups)
        def _(k):
            state_copy(slot, start, width, k).wait_send()

    @pl.loop(1, groups)
    def _(k):
        window_copy(W_D, pack.at[1], devs, k).wait_send()

    for slot, (start, width) in (
        (R_MID, (edge, middle)),
        (R_LOW, pieces_of[S_LOW]),
        (R_HIGH, pieces_of[S_HIGH]),
    ):
        end_back(slot, start, width)


def body(
    row,
    background_realizations,
    realization_expected_data,
    departure_values,
    instrument_dispersion,
    window_piece_offsets,
    window_data_pieces,
    neighbor_piece_ids,
    coupling_indicator,
):
    groups = lax.axis_size("member")
    regions = lax.axis_size("region")
    rows, variable_total = background_realizations.shape
    obs_width = realization_expected_data.shape[1]
    members = groups * rows
    per_device = variable_total // PIECE // groups
    spread = (per_device - 1) // 2
    own_width = per_device * PIECE
    edge = spread * PIECE
    widest = max(edge, own_width - 2 * edge)
    side = neighbor_piece_ids.shape[-1]
    own_count = obs_width // PIECE
    ext_count = own_count + 2 * side
    f32, bf16 = jnp.float32, jnp.bfloat16
    smem = pl.BlockSpec(memory_space=pltpu.SMEM)
    hbm = pl.BlockSpec(memory_space=pl.ANY)
    return pl.pallas_call(
        functools.partial(analysis_kernel, (groups, regions, row, per_device, spread)),
        out_shape=jax.ShapeDtypeStruct((rows, variable_total), f32),
        in_specs=[smem, smem, smem, smem, hbm, hbm, hbm, pl.BlockSpec(memory_space=pltpu.VMEM)],
        out_specs=hbm,
        scratch_shapes=[
            pltpu.VMEM((rows, obs_width), f32),
            pltpu.VMEM((rows, obs_width), f32),
            pltpu.VMEM((own_count, rows, PIECE), f32),
            pltpu.VMEM((own_count, rows, PIECE), f32),
            pltpu.VMEM((ext_count, rows, PIECE), f32),
            pltpu.VMEM((ext_count, rows, PIECE), f32),
            pltpu.VMEM((own_count, 1, PIECE), f32),
            pltpu.VMEM((ext_count, 1, PIECE), f32),
            pltpu.VMEM((2, 2, side, rows, PIECE), f32),
            pltpu.VMEM((2, side, 1, PIECE), f32),
            pltpu.VMEM((2, members, LOCAL), f32),
            pltpu.VMEM((members, LOCAL), f32),
            pltpu.VMEM((members, LOCAL), f32),
            pltpu.VMEM((members, own_width + 2 * edge), f32),
            pltpu.VMEM((LOCAL, members), f32),
            pltpu.VMEM((LOCAL, members), bf16),
            pltpu.VMEM((LOCAL, members), bf16),
            pltpu.VMEM((LOCAL, LOCAL), f32),
            pltpu.VMEM((PIECE, 2 * PIECE), f32),
            pltpu.VMEM((LOCAL, PIECE), f32),
            pltpu.VMEM((LOCAL, LOCAL), f32),
            pltpu.VMEM((members, LOCAL), bf16),
            pltpu.VMEM((members, LOCAL), bf16),
            pltpu.VMEM((LOCAL, own_width + 2 * edge), bf16),
            pltpu.VMEM((LOCAL, own_width + 2 * edge), bf16),
            pltpu.VMEM((members, widest), bf16),
            pltpu.VMEM((members, widest), bf16),
            pltpu.VMEM((members, own_width), f32),
            pltpu.VMEM((2, members, edge), f32),
            pltpu.VMEM((2, members, edge), f32),
            pltpu.VMEM((members, edge), f32),
            pltpu.SemaphoreType.DMA((11, groups)),
            pltpu.SemaphoreType.DMA((11, groups)),
            pltpu.SemaphoreType.DMA((6,)),
            pltpu.SemaphoreType.DMA((6,)),
            pltpu.SemaphoreType.DMA((3, 2)),
            pltpu.SemaphoreType.DMA((3, 2)),
            pltpu.SemaphoreType.DMA((4,)),
        ],
        compiler_params=pltpu.CompilerParams(
            collective_id=0, has_side_effects=True, vmem_limit_bytes=60 * 1024 * 1024
        ),
        name="analysis",
    )(
        window_data_pieces.swapaxes(1, 2),
        neighbor_piece_ids,
        window_piece_offsets,
        coupling_indicator.swapaxes(1, 2),
        background_realizations,
        realization_expected_data,
        departure_values,
        instrument_dispersion.reshape(-1, PIECE),
    )


def row_length(mesh):
    devices = mesh.devices[:, 0].tolist()
    count = len(devices)
    spots = [getattr(d, "coords", None) for d in devices]
    if any(spot is None for spot in spots):
        return count
    row = 1
    while row < count and spots[row][2] == spots[0][2]:
        row += 1
    return row if count % row == 0 else count


def solution(mesh):
    return jax.shard_map(
        functools.partial(body, row_length(mesh)),
        mesh=mesh,
        in_specs=(
            P("member", "region"),
            P("member", "region"),
            P("member", "region"),
            P("region"),
            P("region", None),
            P("region", None, None),
            P("region", None, None),
            P("region", None, None),
        ),
        out_specs=P("member", "region"),
        check_vma=False,
    )
```

```python
import functools

import jax
import jax.numpy as jnp
from jax import lax
from jax.experimental import pallas as pl
from jax.experimental.pallas import tpu as pltpu
from jax.sharding import PartitionSpec as P

PIECE = 128
OBS_PER = 4
LOCAL = OBS_PER * PIECE
TILE = 256

MESH = pl.DeviceIdType.MESH
highest = lax.Precision.HIGHEST


def cols(start, count=1):
    return pl.ds(pl.multiple_of(start * PIECE, PIECE), count * PIECE)


def dot(left, right, contract, precision=None):
    return lax.dot_general(
        left,
        right,
        ((contract[0], contract[1]), ((), ())),
        precision=precision,
        preferred_element_type=jnp.float32,
    )


def at_least(value, bound):
    return jnp.clip(value - bound + 1, 0, 1).astype(jnp.float32)


PLAIN = ((1,), (0,))
BY_ROWS = ((1,), (1,))


def split(value):
    top = value.astype(jnp.bfloat16)
    return top, (value - top.astype(jnp.float32)).astype(jnp.bfloat16)


def factor_block(block, work_ref):
    size = block.shape[0]
    wide = 2 * size
    eye = lax.broadcasted_iota(jnp.int32, (size, size), 0) == lax.broadcasted_iota(
        jnp.int32, (size, size), 1
    )
    work_ref[:, :size] = block
    work_ref[:, size:] = eye.astype(jnp.float32)
    step_rows = 8
    row_ids = lax.broadcasted_iota(jnp.int32, (step_rows, wide), 0)
    for start in range(0, size, step_rows):
        rows = work_ref[start : start + step_rows, :]
        for j in range(step_rows):
            column = rows[:, start + j : start + j + 1]
            scale = 1.0 / jnp.sqrt(column[j : j + 1, :])
            pivot = rows[j : j + 1, :] * scale
            lowered = rows - (column * scale) * pivot
            rows = jnp.where(row_ids > j, lowered, jnp.where(row_ids == j, pivot, rows))
        work_ref[start : start + step_rows, :] = rows
        after = start + step_rows
        if after < size:
            change = dot(rows[:, :size], rows, ((0,), (0,)), highest)
            work_ref[after:, :] = work_ref[after:, :] - change[after:, :]


def snake(index, row, flip):
    return index + (index // row + flip) % 2 * (row - 1 - 2 * (index % row))


def analysis_kernel(
    plan,
    lists_ref,
    ids_ref,
    offsets_ref,
    cover_ref,
    background,
    expected_hbm,
    innov_hbm,
    flat_var,
    out,
    expected,
    innov,
    own_e,
    own_d,
    ext_e,
    ext_d,
    own_var,
    ext_var,
    halo_send,
    var_send,
    pack,
    obs,
    devs,
    states,
    turned,
    turned_top,
    turned_low,
    trailing,
    work,
    lowered,
    panels,
    weight_top,
    weight_low,
    gain_top,
    gain_low,
    state_top,
    state_low,
    result,
    edge_inc,
    edge_got,
    cross_got,
    member_send,
    member_recv,
    pair_send,
    pair_recv,
    back_send,
    back_recv,
    halo_send_sem,
    halo_recv_sem,
    local_sem,
):
    groups, regions, row, per_device, spread = plan
    rows = expected.shape[0]
    own_count = expected.shape[1] // PIECE
    side = ids_ref.shape[2]
    members = groups * rows
    edge = spread * PIECE
    own_width = per_device * PIECE
    middle = own_width - 2 * edge
    me = lax.axis_index("member")
    region = lax.axis_index("region")
    flip = region % 2
    patch = snake(me, row, flip)
    has_dn = patch > 0
    has_up = patch < groups - 1
    near, far = groups // 2 - 1, groups // 2
    is_near, is_far = patch == near, patch == far
    gives_dn = jnp.logical_and(has_dn, patch != far)
    gives_up = jnp.logical_and(has_up, patch != near)
    owner_near = snake(near, row, flip)
    owner_far = snake(far, row, flip)
    lower = groups // 2
    in_lower = me < lower
    member_dn = snake((patch + groups - 1) % groups, row, flip)
    member_up = snake((patch + 1) % groups, row, flip)
    region_after = (region + 1) % regions
    region_before = (region + regions - 1) % regions
    my_rows = pl.ds(pl.multiple_of(me * rows, rows), rows)

    def rows_of(member):
        return pl.ds(pl.multiple_of(member * rows, rows), rows)

    load_e = pltpu.make_async_copy(expected_hbm, expected, local_sem.at[0])
    load_d = pltpu.make_async_copy(innov_hbm, innov, local_sem.at[1])
    load_e.start()
    load_d.start()

    barrier = pltpu.get_barrier_semaphore()
    for k in range(1, groups):
        pl.semaphore_signal(
            barrier, inc=1, device_id=((me + k) % groups, region), device_id_type=MESH
        )
    for other in (region_after, region_before):
        pl.semaphore_signal(barrier, inc=1, device_id=(me, other), device_id_type=MESH)
    pl.semaphore_wait(barrier, groups + 1)

    def state_copy(slot, start, width, k):
        target = (me + k) % groups
        source = snake(target, row, flip) * own_width + start
        return pltpu.make_async_remote_copy(
            src_ref=background.at[:, pl.ds(pl.multiple_of(source, PIECE), width)],
            dst_ref=states.at[my_rows, edge + start : edge + start + width],
            send_sem=member_send.at[slot, k],
            recv_sem=member_recv.at[slot, k],
            device_id=(target, region),
            device_id_type=MESH,
        )

    def state_own(slot, start, width):
        source = patch * own_width + start
        return pltpu.make_async_copy(
            background.at[:, pl.ds(pl.multiple_of(source, PIECE), width)],
            states.at[my_rows, edge + start : edge + start + width],
            member_recv.at[slot, 0],
        )

    def send_states(slot, start, width):
        @pl.loop(1, groups)
        def _(k):
            state_copy(slot, start, width, k).start()

        state_own(slot, start, width).start()

    def take_states(slot, start, width):
        @pl.loop(1, groups)
        def _(k):
            state_copy(slot, start, width, k).wait_recv()

        state_own(slot, start, width).wait()

    def middle_place(way):
        start = (near * own_width + own_width - edge, far * own_width)[way]
        landing = (0, edge + own_width)[way]
        return (
            background.at[:, start : start + edge],
            states.at[my_rows, landing : landing + edge],
        )

    def middle_copy(way, sender):
        source, target = middle_place(way)
        return pltpu.make_async_remote_copy(
            src_ref=source,
            dst_ref=target,
            send_sem=member_send.at[S_X, way],
            recv_sem=member_recv.at[S_X, sender],
            device_id=((owner_far, owner_near)[way], region),
            device_id_type=MESH,
        )

    def middle_own(way):
        return pltpu.make_async_copy(*middle_place(way), local_sem.at[2])

    def send_middle():
        for way, mine in ((0, is_far), (1, is_near)):

            @pl.when(jnp.logical_not(mine))
            def _():
                middle_copy(way, me).start()

            @pl.when(mine)
            def _():
                middle_own(way).start()

    def sent_middle():
        for way, mine in ((0, is_far), (1, is_near)):

            @pl.when(jnp.logical_not(mine))
            def _():
                middle_copy(way, me).wait_send()

    def take_middle(way):
        @pl.loop(1, groups)
        def _(k):
            middle_copy(way, (me + groups - k) % groups).wait_recv()

        middle_own(way).wait()

    def window_copy(slot, source, target_ref, k):
        return pltpu.make_async_remote_copy(
            src_ref=source.at[rows_of((me + k) % groups), :],
            dst_ref=target_ref.at[my_rows, :],
            send_sem=member_send.at[slot, k],
            recv_sem=member_recv.at[slot, k],
            device_id=((me + k) % groups, region),
            device_id_type=MESH,
        )

    def return_copy(slot, start, width, k):
        return pltpu.make_async_remote_copy(
            src_ref=result.at[rows_of((me + k) % groups), start : start + width],
            dst_ref=out.at[
                :, pl.ds(pl.multiple_of(patch * own_width + start, PIECE), width)
            ],
            send_sem=member_send.at[slot, k],
            recv_sem=member_recv.at[slot, k],
            device_id=((me + k) % groups, region),
            device_id_type=MESH,
        )

    def return_own(slot, start, width):
        return pltpu.make_async_copy(
            result.at[my_rows, start : start + width],
            out.at[:, pl.ds(pl.multiple_of(patch * own_width + start, PIECE), width)],
            member_recv.at[slot, 0],
        )

    def returns(slot, p, member):
        if R_LOW <= slot < R_HIGH:
            return jnp.logical_or(p != far, member >= lower)
        if slot >= R_HIGH:
            return jnp.logical_or(p != near, member < lower)
        return p >= 0

    def send_back(slot, start, width):
        @pl.loop(1, groups)
        def _(k):
            @pl.when(returns(slot, patch, (me + k) % groups))
            def _():
                return_copy(slot, start, width, k).start()

        @pl.when(returns(slot, patch, me))
        def _():
            return_own(slot, start, width).start()

    def end_back(slot, start, width):
        @pl.loop(1, groups)
        def _(k):
            @pl.when(returns(slot, patch, (me + k) % groups))
            def _():
                return_copy(slot, start, width, k).wait_send()

            @pl.when(returns(slot, snake((me + groups - k) % groups, row, flip), me))
            def _():
                return_copy(slot, start, width, k).wait_recv()

        @pl.when(returns(slot, patch, me))
        def _():
            return_own(slot, start, width).wait()

    def cross_place(way, member):
        start = (far * own_width, near * own_width + own_width - edge)[way]
        return (
            edge_inc.at[way, rows_of(member), :],
            out.at[:, start : start + edge],
        )

    def cross_copy(way, member):
        source, target = cross_place(way, member)
        return pltpu.make_async_remote_copy(
            src_ref=source,
            dst_ref=target,
            send_sem=member_send.at[R_X, member],
            recv_sem=member_recv.at[R_X, 0],
            device_id=(member, region),
            device_id_type=MESH,
        )

    def cross_own(way):
        return pltpu.make_async_copy(*cross_place(way, me), local_sem.at[3])

    crossing = ((0, is_near, owner_near, 0, lower), (1, is_far, owner_far, lower, groups))

    def send_cross(way):
        first, last = crossing[way][3:]

        @pl.loop(first, last)
        def _(member):
            @pl.when(member != me)
            def _():
                cross_copy(way, member).start()

        @pl.when(jnp.logical_and(me >= first, me < last))
        def _():
            cross_own(way).start()

    def end_cross():
        for way, mine, owner, first, last in crossing:
            inside = jnp.logical_and(me >= first, me < last)

            @pl.when(mine)
            def _():
                @pl.loop(first, last)
                def _(member):
                    @pl.when(member != me)
                    def _():
                        cross_copy(way, member).wait_send()

                @pl.when(inside)
                def _():
                    cross_own(way).wait()

            @pl.when(jnp.logical_and(inside, me != owner))
            def _():
                cross_copy(way, me).wait_recv()

    S_MID, S_NEXT, S_LOW, S_HIGH, W_E, W_D, S_X, R_X, R_MID, R_LOW = range(10)
    R_HIGH = R_LOW + spread
    pieces_of = {
        S_MID: (edge, PIECE),
        S_NEXT: (edge + PIECE, middle - PIECE),
        S_LOW: (0, edge),
        S_HIGH: (own_width - edge, edge),
    }

    send_states(S_MID, *pieces_of[S_MID])

    for load, flat, own, ext in (
        (load_e, expected, own_e, ext_e),
        (load_d, innov, own_d, ext_d),
    ):
        load.wait()
        for n in range(own_count):
            block = flat[:, n * PIECE : (n + 1) * PIECE]
            own[n] = block
            ext[n] = block
    for n in range(own_count):
        own_var[n] = flat_var[n : n + 1, :]
        ext_var[n] = flat_var[n : n + 1, :]
    halo_copies = []
    for part, (own, ext, send) in enumerate(
        ((own_e, ext_e, halo_send.at[0]), (own_var, ext_var, var_send), (own_d, ext_d, halo_send.at[1]))
    ):
        for way, other in ((0, region_after), (1, region_before)):
            for k in range(side):
                send[way, k] = own[ids_ref[0, way, k]]
            landing = own_count + way * side
            copy = pltpu.make_async_remote_copy(
                src_ref=send.at[way],
                dst_ref=ext.at[landing : landing + side],
                send_sem=halo_send_sem.at[part, way],
                recv_sem=halo_recv_sem.at[part, way],
                device_id=(me, other),
                device_id_type=MESH,
            )
            copy.start()
            halo_copies.append(copy)

    def pack_window(ext, buffer, k):
        target = (me + k) % groups
        p = snake(target, row, flip)
        for n in range(OBS_PER):
            buffer[rows_of(target), n * PIECE : (n + 1) * PIECE] = ext[lists_ref[0, n, p]]

    for copy in halo_copies[:2]:
        copy.wait_recv()

    @pl.loop(1, groups)
    def _(k):
        pack_window(ext_e, pack.at[0], k)
        window_copy(W_E, pack.at[0], obs, k).start()

    pack_window(ext_e, obs, 0)
    for copy in halo_copies[2:]:
        copy.wait_recv()
    variances = [ext_var[lists_ref[0, n, patch]] for n in range(OBS_PER)]

    @pl.loop(1, groups)
    def _(k):
        pack_window(ext_d, pack.at[1], k)

    pack_window(ext_d, devs, 0)

    @pl.loop(1, groups)
    def _(k):
        window_copy(W_E, pack.at[0], obs, k).wait_send()

    send_states(S_LOW, *pieces_of[S_LOW])
    send_middle()
    send_states(S_HIGH, *pieces_of[S_HIGH])

    @pl.loop(1, groups)
    def _(k):
        window_copy(W_E, pack.at[0], obs, k).wait_recv()

    tiles = members // PIECE

    def add_rows(t, total):
        part = obs[pl.ds(pl.multiple_of(t * PIECE, PIECE), PIECE), :]
        return total + jnp.sum(part, axis=0, keepdims=True)

    mean = lax.fori_loop(0, tiles, add_rows, jnp.zeros((1, LOCAL), jnp.float32)) / members

    @pl.loop(0, tiles)
    def _(t):
        place = pl.ds(pl.multiple_of(t * PIECE, PIECE), PIECE)
        part = obs[place, :] - mean
        obs[place, :] = part
        flat = part.T
        turned[:, place] = flat
        top, low = split(flat)
        turned_top[:, place] = top
        turned_low[:, place] = low

    @pl.loop(0, LOCAL // TILE)
    def _(i):
        place = pl.ds(pl.multiple_of(i * TILE, TILE), TILE)

        @pl.loop(0, LOCAL // TILE)
        def _(j):
            other = pl.ds(pl.multiple_of(j * TILE, TILE), TILE)
            trailing[place, other] = dot(
                turned[place, :], obs[:, other], PLAIN, highest
            ) / (members - 1.0)

    eye = lax.broadcasted_iota(jnp.int32, (PIECE, PIECE), 0) == lax.broadcasted_iota(
        jnp.int32, (PIECE, PIECE), 1
    )
    for n in range(OBS_PER):
        place = slice(n * PIECE, (n + 1) * PIECE)
        trailing[place, place] = trailing[place, place] + jnp.where(eye, variances[n], 0.0)

    def forward(way):
        start, other = ((edge, member_dn), (own_width, member_up))[way]
        landing = (edge + own_width, 0)[way]
        return pltpu.make_async_remote_copy(
            src_ref=states.at[:, start : start + edge],
            dst_ref=states.at[:, landing : landing + edge],
            send_sem=pair_send.at[way],
            recv_sem=pair_recv.at[way],
            device_id=(other, region),
            device_id_type=MESH,
        )

    def backward(way, b):
        other = (member_up, member_dn)[way]
        at = slice(b * PIECE, (b + 1) * PIECE)
        return pltpu.make_async_remote_copy(
            src_ref=edge_inc.at[way, :, at],
            dst_ref=edge_got.at[way, :, at],
            send_sem=back_send.at[way, b],
            recv_sem=back_recv.at[way, b],
            device_id=(other, region),
            device_id_type=MESH,
        )

    line = lax.broadcasted_iota(jnp.int32, (LOCAL, PIECE), 0)
    for n in range(OBS_PER):
        place = slice(n * PIECE, (n + 1) * PIECE)
        lowered[place, :] = jnp.zeros((PIECE, LOCAL), jnp.float32)
        lowered[place, place] = eye.astype(jnp.float32)

    @pl.loop(0, OBS_PER)
    def _(k):
        place = cols(k)
        @pl.when(k == 2)
        def _():
            @pl.loop(1, groups)
            def _(j):
                window_copy(W_D, pack.at[1], devs, j).start()

            take_states(S_LOW, *pieces_of[S_LOW])

            @pl.when(gives_dn)
            def _():
                forward(0).start()

        @pl.when(k == 3)
        def _():
            take_states(S_HIGH, *pieces_of[S_HIGH])

            @pl.when(gives_up)
            def _():
                forward(1).start()

        factor_block(trailing[place, place], work)

        inverse = work[:, PIECE:]
        lowered[place, :] = dot(inverse, lowered[place, :], PLAIN, highest)
        panel = dot(trailing[:, place], inverse, BY_ROWS, highest)
        panel = jnp.where(line >= (k + 1) * PIECE, panel, 0.0)
        panels[...] = panel

        @pl.loop(0, LOCAL // PIECE)
        def _(i):
            part = cols(i)
            trailing[part, :] = trailing[part, :] - dot(
                panels[part, :], panels[...], BY_ROWS, highest
            )
            lowered[part, :] = lowered[part, :] - dot(
                panels[part, :], lowered[place, :], PLAIN, highest
            )

    blocks_total = cover_ref.shape[2]

    def find_gain(start, width):
        def add_states(t, total):
            part = states[
                pl.ds(pl.multiple_of(t * PIECE, PIECE), PIECE), start : start + width
            ]
            return total + jnp.sum(part, axis=0, keepdims=True)

        centre = (
            lax.fori_loop(0, tiles, add_states, jnp.zeros((1, width), jnp.float32))
            / members
        )

        @pl.loop(0, tiles)
        def _(t):
            place = pl.ds(pl.multiple_of(t * PIECE, PIECE), PIECE)
            top, low = split(states[place, start : start + width] - centre)
            state_top[place, :width] = top
            state_low[place, :width] = low

        first = patch * per_device - spread + start // PIECE

        @pl.loop(0, OBS_PER)
        def _(n):
            place = cols(n)
            left_top, left_low = turned_top[place, :], turned_low[place, :]
            right_top, right_low = state_top[:, :width], state_low[:, :width]
            gain = (
                dot(left_top, right_top, PLAIN)
                + dot(left_top, right_low, PLAIN)
                + dot(left_low, right_top, PLAIN)
            ) / (members - 1.0)
            for b in range(width // PIECE):
                at = slice(b * PIECE, (b + 1) * PIECE)
                spot = jnp.clip(first + b, 0, blocks_total - 1)
                top, low = split(gain[:, at] * cover_ref[0, n, spot].astype(jnp.float32))
                gain_top[place, start + b * PIECE : start + (b + 1) * PIECE] = top
                gain_low[place, start + b * PIECE : start + (b + 1) * PIECE] = low

    send_states(S_NEXT, *pieces_of[S_NEXT])

    @pl.loop(0, LOCAL // PIECE)
    def _(i):
        part = cols(i)
        trailing[part, :] = dot(lowered[:, part].T, lowered[...], PLAIN, highest)

    find_gain(edge, edge)
    find_gain(own_width, edge)
    take_states(S_MID, *pieces_of[S_MID])
    find_gain(edge + edge, PIECE)

    @pl.when(has_up)
    def _():
        @pl.when(gives_up)
        def _():
            forward(0).wait_recv()

        @pl.when(is_near)
        def _():
            take_middle(1)

        find_gain(edge + own_width, edge)


    @pl.loop(1, groups)
    def _(k):
        window_copy(W_D, pack.at[1], devs, k).wait_recv()

    @pl.loop(0, members // TILE)
    def _(t):
        place = pl.ds(pl.multiple_of(t * TILE, TILE), TILE)
        top, low = split(dot(devs[place, :], trailing[...], PLAIN, highest))
        weight_top[place, :] = top
        weight_low[place, :] = low

    def increments(start, width, store):
        @pl.loop(0, members // TILE)
        def _(t):
            place = pl.ds(pl.multiple_of(t * TILE, TILE), TILE)
            left_top, left_low = weight_top[place, :], weight_low[place, :]
            right_top = gain_top[:, start : start + width]
            right_low = gain_low[:, start : start + width]
            store(
                place,
                dot(left_top, right_top, PLAIN)
                + dot(left_top, right_low, PLAIN)
                + dot(left_low, right_top, PLAIN),
            )

    def own_part(start, width):
        def store(place, value):
            result[place, start : start + width] = (
                states[place, edge + start : edge + start + width] + value
            )

        increments(edge + start, width, store)

    def other_part(way):
        place_in = (edge + own_width, 0)[way]

        def store(place, value):
            edge_inc[way, place, :] = states[place, place_in : place_in + edge] + value

        increments(place_in, edge, store)

    def foreign(way, owner, b):
        start = (0, own_width - edge)[way]
        bound = offsets_ref[0, owner + way] - owner * per_device
        block = start // PIECE + b
        return at_least(bound, block + 1) if way == 0 else at_least(block, bound)

    half_rows = lower * rows

    def settle(way, b, first=0, last=members):
        start = (0, own_width - edge)[way]
        share = foreign(way, patch, b)
        at = slice(start + b * PIECE, start + (b + 1) * PIECE)

        @pl.loop(first // PIECE, last // PIECE)
        def _(t):
            place = pl.ds(pl.multiple_of(t * PIECE, PIECE), PIECE)
            theirs = edge_got[way, place, b * PIECE : (b + 1) * PIECE]
            result[place, at] = theirs * share + result[place, at] * (1.0 - share)

    def settle_cross(way, owner, first, last):
        @pl.loop(first // PIECE, last // PIECE)
        def _(t):
            place = pl.ds(pl.multiple_of(t * PIECE, PIECE), PIECE)
            for b in range(spread):
                share = foreign(way, owner, b)
                at = slice(b * PIECE, (b + 1) * PIECE)
                mine = edge_inc[way, place, at]
                theirs = cross_got[place, at]
                edge_inc[way, place, at] = mine * share + theirs * (1.0 - share)

    def swap(near_sends, part):
        first = half_rows if near_sends else 0
        count = members - half_rows if near_sends else half_rows
        sent = slice(first, first + count)
        if part == 0:
            way = 0 if near_sends else 1
            source = edge_inc.at[way, sent, :]
            target = edge_got.at[way, sent, :]
        else:
            start = own_width - edge if near_sends else 0
            source = result.at[sent, start : start + edge]
            target = cross_got.at[sent, :]
        return pltpu.make_async_remote_copy(
            src_ref=source,
            dst_ref=target,
            send_sem=pair_send.at[4 + part],
            recv_sem=pair_recv.at[4 + part],
            device_id=(owner_far if near_sends else owner_near, region),
            device_id_type=MESH,
        )

    @pl.when(has_up)
    def _():
        other_part(0)

        @pl.when(gives_up)
        def _():
            for b in range(spread):
                backward(0, b).start()

        @pl.when(is_near)
        def _():
            swap(True, 0).start()

    take_states(S_NEXT, *pieces_of[S_NEXT])
    find_gain(edge + edge + PIECE, middle - PIECE)
    own_part(edge, middle)
    send_back(R_MID, edge, middle)
    @pl.when(has_dn)
    def _():
        @pl.when(gives_dn)
        def _():
            forward(1).wait_recv()

        @pl.when(is_far)
        def _():
            take_middle(0)

        find_gain(0, edge)
        other_part(1)

        @pl.when(gives_dn)
        def _():
            for b in range(spread):
                backward(1, b).start()

        @pl.when(is_far)
        def _():
            swap(False, 0).start()

    own_part(0, edge)

    @pl.when(is_far)
    def _():
        swap(False, 1).start()

    own_part(own_width - edge, edge)

    @pl.when(is_near)
    def _():
        swap(True, 1).start()

    @pl.when(is_far)
    def _():
        swap(True, 0).wait_recv()

    @pl.when(is_near)
    def _():
        swap(False, 0).wait_recv()

    for b in range(spread):

        @pl.when(gives_dn)
        def _():
            backward(0, b).wait_recv()
            settle(0, b)

        @pl.when(is_far)
        def _():
            settle(0, b, half_rows, members)

        send_back(R_LOW + b, b * PIECE, PIECE)

        @pl.when(gives_up)
        def _():
            backward(1, b).wait_recv()
            settle(1, b)

        @pl.when(is_near)
        def _():
            settle(1, b, 0, half_rows)

        send_back(R_HIGH + b, own_width - edge + b * PIECE, PIECE)

    @pl.when(is_near)
    def _():
        swap(True, 0).wait_send()
        swap(False, 1).wait_recv()
        settle_cross(0, far, 0, half_rows)
        send_cross(0)

    @pl.when(is_far)
    def _():
        swap(False, 0).wait_send()
        swap(True, 1).wait_recv()
        settle_cross(1, near, half_rows, members)
        send_cross(1)

    for copy in halo_copies:
        copy.wait_send()

    @pl.when(gives_dn)
    def _():
        forward(0).wait_send()
        for b in range(spread):
            backward(1, b).wait_send()

    @pl.when(gives_up)
    def _():
        forward(1).wait_send()
        for b in range(spread):
            backward(0, b).wait_send()

    @pl.when(is_near)
    def _():
        swap(True, 1).wait_send()

    @pl.when(is_far)
    def _():
        swap(False, 1).wait_send()

    sent_middle()
    end_cross()

    for slot, (start, width) in pieces_of.items():

        @pl.loop(1, groups)
        def _(k):
            state_copy(slot, start, width, k).wait_send()

    @pl.loop(1, groups)
    def _(k):
        window_copy(W_D, pack.at[1], devs, k).wait_send()

    end_back(R_MID, edge, middle)
    for b in range(spread):
        end_back(R_LOW + b, b * PIECE, PIECE)
        end_back(R_HIGH + b, own_width - edge + b * PIECE, PIECE)


def body(
    row,
    background_realizations,
    realization_expected_data,
    departure_values,
    instrument_dispersion,
    window_piece_offsets,
    window_data_pieces,
    neighbor_piece_ids,
    coupling_indicator,
):
    groups = lax.axis_size("member")
    regions = lax.axis_size("region")
    rows, variable_total = background_realizations.shape
    obs_width = realization_expected_data.shape[1]
    members = groups * rows
    per_device = variable_total // PIECE // groups
    spread = (per_device - 1) // 2
    own_width = per_device * PIECE
    edge = spread * PIECE
    widest = max(edge, own_width - 2 * edge)
    side = neighbor_piece_ids.shape[-1]
    own_count = obs_width // PIECE
    ext_count = own_count + 2 * side
    f32, bf16 = jnp.float32, jnp.bfloat16
    smem = pl.BlockSpec(memory_space=pltpu.SMEM)
    hbm = pl.BlockSpec(memory_space=pl.ANY)
    return pl.pallas_call(
        functools.partial(analysis_kernel, (groups, regions, row, per_device, spread)),
        out_shape=jax.ShapeDtypeStruct((rows, variable_total), f32),
        in_specs=[smem, smem, smem, smem, hbm, hbm, hbm, pl.BlockSpec(memory_space=pltpu.VMEM)],
        out_specs=hbm,
        scratch_shapes=[
            pltpu.VMEM((rows, obs_width), f32),
            pltpu.VMEM((rows, obs_width), f32),
            pltpu.VMEM((own_count, rows, PIECE), f32),
            pltpu.VMEM((own_count, rows, PIECE), f32),
            pltpu.VMEM((ext_count, rows, PIECE), f32),
            pltpu.VMEM((ext_count, rows, PIECE), f32),
            pltpu.VMEM((own_count, 1, PIECE), f32),
            pltpu.VMEM((ext_count, 1, PIECE), f32),
            pltpu.VMEM((2, 2, side, rows, PIECE), f32),
            pltpu.VMEM((2, side, 1, PIECE), f32),
            pltpu.VMEM((2, members, LOCAL), f32),
            pltpu.VMEM((members, LOCAL), f32),
            pltpu.VMEM((members, LOCAL), f32),
            pltpu.VMEM((members, own_width + 2 * edge), f32),
            pltpu.VMEM((LOCAL, members), f32),
            pltpu.VMEM((LOCAL, members), bf16),
            pltpu.VMEM((LOCAL, members), bf16),
            pltpu.VMEM((LOCAL, LOCAL), f32),
            pltpu.VMEM((PIECE, 2 * PIECE), f32),
            pltpu.VMEM((LOCAL, LOCAL), f32),
            pltpu.VMEM((LOCAL, PIECE), f32),
            pltpu.VMEM((members, LOCAL), bf16),
            pltpu.VMEM((members, LOCAL), bf16),
            pltpu.VMEM((LOCAL, own_width + 2 * edge), bf16),
            pltpu.VMEM((LOCAL, own_width + 2 * edge), bf16),
            pltpu.VMEM((members, widest), bf16),
            pltpu.VMEM((members, widest), bf16),
            pltpu.VMEM((members, own_width), f32),
            pltpu.VMEM((2, members, edge), f32),
            pltpu.VMEM((2, members, edge), f32),
            pltpu.VMEM((members, edge), f32),
            pltpu.SemaphoreType.DMA((9 + 2 * spread, groups)),
            pltpu.SemaphoreType.DMA((9 + 2 * spread, groups)),
            pltpu.SemaphoreType.DMA((6,)),
            pltpu.SemaphoreType.DMA((6,)),
            pltpu.SemaphoreType.DMA((2, spread)),
            pltpu.SemaphoreType.DMA((2, spread)),
            pltpu.SemaphoreType.DMA((3, 2)),
            pltpu.SemaphoreType.DMA((3, 2)),
            pltpu.SemaphoreType.DMA((4,)),
        ],
        compiler_params=pltpu.CompilerParams(
            collective_id=0, has_side_effects=True, vmem_limit_bytes=60 * 1024 * 1024
        ),
        name="analysis",
    )(
        window_data_pieces.swapaxes(1, 2),
        neighbor_piece_ids,
        window_piece_offsets,
        coupling_indicator.swapaxes(1, 2),
        background_realizations,
        realization_expected_data,
        departure_values,
        instrument_dispersion.reshape(-1, PIECE),
    )


def row_length(mesh):
    devices = mesh.devices[:, 0].tolist()
    count = len(devices)
    spots = [getattr(d, "coords", None) for d in devices]
    if any(spot is None for spot in spots):
        return count
    row = 1
    while row < count and spots[row][2] == spots[0][2]:
        row += 1
    return row if count % row == 0 else count


def solution(mesh):
    return jax.shard_map(
        functools.partial(body, row_length(mesh)),
        mesh=mesh,
        in_specs=(
            P("member", "region"),
            P("member", "region"),
            P("member", "region"),
            P("region"),
            P("region", None),
            P("region", None, None),
            P("region", None, None),
            P("region", None, None),
        ),
        out_specs=P("member", "region"),
        check_vma=False,
    )
```

```python
import functools

import jax
import jax.numpy as jnp
from jax import lax
from jax.experimental import pallas as pl
from jax.experimental.pallas import tpu as pltpu
from jax.sharding import PartitionSpec as P

PIECE = 128
OBS_PER = 4
LOCAL = OBS_PER * PIECE
TILE = 256

MESH = pl.DeviceIdType.MESH
highest = lax.Precision.HIGHEST


def cols(start, count=1):
    return pl.ds(pl.multiple_of(start * PIECE, PIECE), count * PIECE)


def dot(left, right, contract, precision=None):
    return lax.dot_general(
        left,
        right,
        ((contract[0], contract[1]), ((), ())),
        precision=precision,
        preferred_element_type=jnp.float32,
    )


def at_least(value, bound):
    return jnp.clip(value - bound + 1, 0, 1).astype(jnp.float32)


PLAIN = ((1,), (0,))
BY_ROWS = ((1,), (1,))


def split(value):
    top = value.astype(jnp.bfloat16)
    return top, (value - top.astype(jnp.float32)).astype(jnp.bfloat16)


def factor_block(block, work_ref):
    size = block.shape[0]
    wide = 2 * size
    eye = lax.broadcasted_iota(jnp.int32, (size, size), 0) == lax.broadcasted_iota(
        jnp.int32, (size, size), 1
    )
    work_ref[:, :size] = block
    work_ref[:, size:] = eye.astype(jnp.float32)
    step_rows = 8
    row_ids = lax.broadcasted_iota(jnp.int32, (step_rows, wide), 0)
    for start in range(0, size, step_rows):
        rows = work_ref[start : start + step_rows, :]
        for j in range(step_rows):
            column = rows[:, start + j : start + j + 1]
            scale = 1.0 / jnp.sqrt(column[j : j + 1, :])
            pivot = rows[j : j + 1, :] * scale
            lowered = rows - (column * scale) * pivot
            rows = jnp.where(row_ids > j, lowered, jnp.where(row_ids == j, pivot, rows))
        work_ref[start : start + step_rows, :] = rows
        after = start + step_rows
        if after < size:
            change = dot(rows[:, :size], rows, ((0,), (0,)), highest)
            work_ref[after:, :] = work_ref[after:, :] - change[after:, :]


def snake(index, row, flip):
    return index + (index // row + flip) % 2 * (row - 1 - 2 * (index % row))


def analysis_kernel(
    plan,
    lists_ref,
    ids_ref,
    offsets_ref,
    cover_ref,
    background,
    expected_hbm,
    innov_hbm,
    flat_var,
    out,
    expected,
    innov,
    own_e,
    own_d,
    ext_e,
    ext_d,
    own_var,
    ext_var,
    halo_send,
    var_send,
    pack,
    obs,
    devs,
    states,
    turned,
    turned_top,
    turned_low,
    trailing,
    work,
    lowered,
    panels,
    weight_top,
    weight_low,
    gain_top,
    gain_low,
    state_top,
    state_low,
    result,
    edge_inc,
    edge_got,
    cross_got,
    member_send,
    member_recv,
    pair_send,
    pair_recv,
    back_send,
    back_recv,
    halo_send_sem,
    halo_recv_sem,
    local_sem,
):
    groups, regions, row, per_device, spread = plan
    rows = expected.shape[0]
    own_count = expected.shape[1] // PIECE
    side = ids_ref.shape[2]
    members = groups * rows
    edge = spread * PIECE
    own_width = per_device * PIECE
    middle = own_width - 2 * edge
    me = lax.axis_index("member")
    region = lax.axis_index("region")
    flip = region % 2
    patch = snake(me, row, flip)
    has_dn = patch > 0
    has_up = patch < groups - 1
    near, far = groups // 2 - 1, groups // 2
    is_near, is_far = patch == near, patch == far
    gives_dn = jnp.logical_and(has_dn, patch != far)
    gives_up = jnp.logical_and(has_up, patch != near)
    owner_near = snake(near, row, flip)
    owner_far = snake(far, row, flip)
    lower = groups // 2
    in_lower = me < lower
    member_dn = snake((patch + groups - 1) % groups, row, flip)
    member_up = snake((patch + 1) % groups, row, flip)
    region_after = (region + 1) % regions
    region_before = (region + regions - 1) % regions
    my_rows = pl.ds(pl.multiple_of(me * rows, rows), rows)

    def rows_of(member):
        return pl.ds(pl.multiple_of(member * rows, rows), rows)

    load_e = pltpu.make_async_copy(expected_hbm, expected, local_sem.at[0])
    load_d = pltpu.make_async_copy(innov_hbm, innov, local_sem.at[1])
    load_e.start()
    load_d.start()

    barrier = pltpu.get_barrier_semaphore()
    for k in range(1, groups):
        pl.semaphore_signal(
            barrier, inc=1, device_id=((me + k) % groups, region), device_id_type=MESH
        )
    for other in (region_after, region_before):
        pl.semaphore_signal(barrier, inc=1, device_id=(me, other), device_id_type=MESH)
    pl.semaphore_wait(barrier, groups + 1)

    def state_copy(slot, start, width, k):
        target = (me + k) % groups
        source = snake(target, row, flip) * own_width + start
        return pltpu.make_async_remote_copy(
            src_ref=background.at[:, pl.ds(pl.multiple_of(source, PIECE), width)],
            dst_ref=states.at[my_rows, edge + start : edge + start + width],
            send_sem=member_send.at[slot, k],
            recv_sem=member_recv.at[slot, k],
            device_id=(target, region),
            device_id_type=MESH,
        )

    def state_own(slot, start, width):
        source = patch * own_width + start
        return pltpu.make_async_copy(
            background.at[:, pl.ds(pl.multiple_of(source, PIECE), width)],
            states.at[my_rows, edge + start : edge + start + width],
            member_recv.at[slot, 0],
        )

    def send_states(slot, start, width):
        @pl.loop(1, groups)
        def _(k):
            state_copy(slot, start, width, k).start()

        state_own(slot, start, width).start()

    def take_states(slot, start, width):
        @pl.loop(1, groups)
        def _(k):
            state_copy(slot, start, width, k).wait_recv()

        state_own(slot, start, width).wait()

    def middle_place(way):
        start = (near * own_width + own_width - edge, far * own_width)[way]
        landing = (0, edge + own_width)[way]
        return (
            background.at[:, start : start + edge],
            states.at[my_rows, landing : landing + edge],
        )

    def middle_copy(way, sender):
        source, target = middle_place(way)
        return pltpu.make_async_remote_copy(
            src_ref=source,
            dst_ref=target,
            send_sem=member_send.at[S_X, way],
            recv_sem=member_recv.at[S_X, sender],
            device_id=((owner_far, owner_near)[way], region),
            device_id_type=MESH,
        )

    def middle_own(way):
        return pltpu.make_async_copy(*middle_place(way), local_sem.at[2])

    def send_middle():
        for way, mine in ((0, is_far), (1, is_near)):

            @pl.when(jnp.logical_not(mine))
            def _():
                middle_copy(way, me).start()

            @pl.when(mine)
            def _():
                middle_own(way).start()

    def sent_middle():
        for way, mine in ((0, is_far), (1, is_near)):

            @pl.when(jnp.logical_not(mine))
            def _():
                middle_copy(way, me).wait_send()

    def take_middle(way):
        @pl.loop(1, groups)
        def _(k):
            middle_copy(way, (me + groups - k) % groups).wait_recv()

        middle_own(way).wait()

    def window_copy(slot, source, target_ref, k):
        return pltpu.make_async_remote_copy(
            src_ref=source.at[rows_of((me + k) % groups), :],
            dst_ref=target_ref.at[my_rows, :],
            send_sem=member_send.at[slot, k],
            recv_sem=member_recv.at[slot, k],
            device_id=((me + k) % groups, region),
            device_id_type=MESH,
        )

    def return_copy(slot, start, width, k):
        return pltpu.make_async_remote_copy(
            src_ref=result.at[rows_of((me + k) % groups), start : start + width],
            dst_ref=out.at[
                :, pl.ds(pl.multiple_of(patch * own_width + start, PIECE), width)
            ],
            send_sem=member_send.at[slot, k],
            recv_sem=member_recv.at[slot, k],
            device_id=((me + k) % groups, region),
            device_id_type=MESH,
        )

    def return_own(slot, start, width):
        return pltpu.make_async_copy(
            result.at[my_rows, start : start + width],
            out.at[:, pl.ds(pl.multiple_of(patch * own_width + start, PIECE), width)],
            member_recv.at[slot, 0],
        )

    def returns(slot, p, member):
        if R_LOW <= slot < R_HIGH:
            return jnp.logical_or(p != far, member >= lower)
        if slot >= R_HIGH:
            return jnp.logical_or(p != near, member < lower)
        return p >= 0

    def send_back(slot, start, width):
        @pl.loop(1, groups)
        def _(k):
            @pl.when(returns(slot, patch, (me + k) % groups))
            def _():
                return_copy(slot, start, width, k).start()

        @pl.when(returns(slot, patch, me))
        def _():
            return_own(slot, start, width).start()

    def end_back(slot, start, width):
        @pl.loop(1, groups)
        def _(k):
            @pl.when(returns(slot, patch, (me + k) % groups))
            def _():
                return_copy(slot, start, width, k).wait_send()

            @pl.when(returns(slot, snake((me + groups - k) % groups, row, flip), me))
            def _():
                return_copy(slot, start, width, k).wait_recv()

        @pl.when(returns(slot, patch, me))
        def _():
            return_own(slot, start, width).wait()

    def cross_place(way, member):
        start = (far * own_width, near * own_width + own_width - edge)[way]
        return (
            edge_inc.at[way, rows_of(member), :],
            out.at[:, start : start + edge],
        )

    def cross_copy(way, member):
        source, target = cross_place(way, member)
        return pltpu.make_async_remote_copy(
            src_ref=source,
            dst_ref=target,
            send_sem=member_send.at[R_X, member],
            recv_sem=member_recv.at[R_X, 0],
            device_id=(member, region),
            device_id_type=MESH,
        )

    def cross_own(way):
        return pltpu.make_async_copy(*cross_place(way, me), local_sem.at[3])

    crossing = ((0, is_near, owner_near, 0, lower), (1, is_far, owner_far, lower, groups))

    def send_cross(way):
        first, last = crossing[way][3:]

        @pl.loop(first, last)
        def _(member):
            @pl.when(member != me)
            def _():
                cross_copy(way, member).start()

        @pl.when(jnp.logical_and(me >= first, me < last))
        def _():
            cross_own(way).start()

    def end_cross():
        for way, mine, owner, first, last in crossing:
            inside = jnp.logical_and(me >= first, me < last)

            @pl.when(mine)
            def _():
                @pl.loop(first, last)
                def _(member):
                    @pl.when(member != me)
                    def _():
                        cross_copy(way, member).wait_send()

                @pl.when(inside)
                def _():
                    cross_own(way).wait()

            @pl.when(jnp.logical_and(inside, me != owner))
            def _():
                cross_copy(way, me).wait_recv()

    S_MID, S_NEXT, S_LOW, S_HIGH, W_E, W_D, S_X, R_X, R_MID, R_NEXT, R_LOW = range(11)
    R_HIGH = R_LOW + spread
    pieces_of = {
        S_MID: (edge, PIECE),
        S_NEXT: (edge + PIECE, middle - PIECE),
        S_LOW: (0, edge),
        S_HIGH: (own_width - edge, edge),
    }

    send_states(S_MID, *pieces_of[S_MID])

    for load, flat, own, ext in (
        (load_e, expected, own_e, ext_e),
        (load_d, innov, own_d, ext_d),
    ):
        load.wait()
        for n in range(own_count):
            block = flat[:, n * PIECE : (n + 1) * PIECE]
            own[n] = block
            ext[n] = block
    for n in range(own_count):
        own_var[n] = flat_var[n : n + 1, :]
        ext_var[n] = flat_var[n : n + 1, :]
    halo_copies = []
    for part, (own, ext, send) in enumerate(
        ((own_e, ext_e, halo_send.at[0]), (own_var, ext_var, var_send), (own_d, ext_d, halo_send.at[1]))
    ):
        for way, other in ((0, region_after), (1, region_before)):
            for k in range(side):
                send[way, k] = own[ids_ref[0, way, k]]
            landing = own_count + way * side
            copy = pltpu.make_async_remote_copy(
                src_ref=send.at[way],
                dst_ref=ext.at[landing : landing + side],
                send_sem=halo_send_sem.at[part, way],
                recv_sem=halo_recv_sem.at[part, way],
                device_id=(me, other),
                device_id_type=MESH,
            )
            copy.start()
            halo_copies.append(copy)

    def pack_window(ext, buffer, k):
        target = (me + k) % groups
        p = snake(target, row, flip)
        for n in range(OBS_PER):
            buffer[rows_of(target), n * PIECE : (n + 1) * PIECE] = ext[lists_ref[0, n, p]]

    for copy in halo_copies[:2]:
        copy.wait_recv()

    @pl.loop(1, groups)
    def _(k):
        pack_window(ext_e, pack.at[0], k)
        window_copy(W_E, pack.at[0], obs, k).start()

    pack_window(ext_e, obs, 0)
    for copy in halo_copies[2:]:
        copy.wait_recv()
    variances = [ext_var[lists_ref[0, n, patch]] for n in range(OBS_PER)]

    @pl.loop(1, groups)
    def _(k):
        pack_window(ext_d, pack.at[1], k)

    pack_window(ext_d, devs, 0)

    @pl.loop(1, groups)
    def _(k):
        window_copy(W_E, pack.at[0], obs, k).wait_send()

    send_states(S_LOW, *pieces_of[S_LOW])
    send_middle()
    send_states(S_HIGH, *pieces_of[S_HIGH])

    @pl.loop(1, groups)
    def _(k):
        window_copy(W_E, pack.at[0], obs, k).wait_recv()

    tiles = members // PIECE

    def add_rows(t, total):
        part = obs[pl.ds(pl.multiple_of(t * PIECE, PIECE), PIECE), :]
        return total + jnp.sum(part, axis=0, keepdims=True)

    mean = lax.fori_loop(0, tiles, add_rows, jnp.zeros((1, LOCAL), jnp.float32)) / members

    @pl.loop(0, tiles)
    def _(t):
        place = pl.ds(pl.multiple_of(t * PIECE, PIECE), PIECE)
        part = obs[place, :] - mean
        obs[place, :] = part
        flat = part.T
        turned[:, place] = flat
        top, low = split(flat)
        turned_top[:, place] = top
        turned_low[:, place] = low

    @pl.loop(0, LOCAL // TILE)
    def _(i):
        place = pl.ds(pl.multiple_of(i * TILE, TILE), TILE)

        @pl.loop(0, LOCAL // TILE)
        def _(j):
            other = pl.ds(pl.multiple_of(j * TILE, TILE), TILE)
            trailing[place, other] = dot(
                turned[place, :], obs[:, other], PLAIN, highest
            ) / (members - 1.0)

    eye = lax.broadcasted_iota(jnp.int32, (PIECE, PIECE), 0) == lax.broadcasted_iota(
        jnp.int32, (PIECE, PIECE), 1
    )
    for n in range(OBS_PER):
        place = slice(n * PIECE, (n + 1) * PIECE)
        trailing[place, place] = trailing[place, place] + jnp.where(eye, variances[n], 0.0)

    def forward(way):
        start, other = ((edge, member_dn), (own_width, member_up))[way]
        landing = (edge + own_width, 0)[way]
        return pltpu.make_async_remote_copy(
            src_ref=states.at[:, start : start + edge],
            dst_ref=states.at[:, landing : landing + edge],
            send_sem=pair_send.at[way],
            recv_sem=pair_recv.at[way],
            device_id=(other, region),
            device_id_type=MESH,
        )

    def backward(way, b):
        other = (member_up, member_dn)[way]
        at = slice(b * PIECE, (b + 1) * PIECE)
        return pltpu.make_async_remote_copy(
            src_ref=edge_inc.at[way, :, at],
            dst_ref=edge_got.at[way, :, at],
            send_sem=back_send.at[way, b],
            recv_sem=back_recv.at[way, b],
            device_id=(other, region),
            device_id_type=MESH,
        )

    line = lax.broadcasted_iota(jnp.int32, (LOCAL, PIECE), 0)
    for n in range(OBS_PER):
        place = slice(n * PIECE, (n + 1) * PIECE)
        lowered[place, :] = jnp.zeros((PIECE, LOCAL), jnp.float32)
        lowered[place, place] = eye.astype(jnp.float32)

    @pl.loop(0, OBS_PER)
    def _(k):
        place = cols(k)
        @pl.when(k == 2)
        def _():
            @pl.loop(1, groups)
            def _(j):
                window_copy(W_D, pack.at[1], devs, j).start()

            take_states(S_LOW, *pieces_of[S_LOW])

            @pl.when(gives_dn)
            def _():
                forward(0).start()

        @pl.when(k == 3)
        def _():
            take_states(S_HIGH, *pieces_of[S_HIGH])

            @pl.when(gives_up)
            def _():
                forward(1).start()

            send_states(S_NEXT, *pieces_of[S_NEXT])

        factor_block(trailing[place, place], work)

        inverse = work[:, PIECE:]
        lowered[place, :] = dot(inverse, lowered[place, :], PLAIN, highest)
        panel = dot(trailing[:, place], inverse, BY_ROWS, highest)
        panel = jnp.where(line >= (k + 1) * PIECE, panel, 0.0)
        panels[...] = panel

        @pl.loop(0, LOCAL // PIECE)
        def _(i):
            part = cols(i)
            trailing[part, :] = trailing[part, :] - dot(
                panels[part, :], panels[...], BY_ROWS, highest
            )
            lowered[part, :] = lowered[part, :] - dot(
                panels[part, :], lowered[place, :], PLAIN, highest
            )

    blocks_total = cover_ref.shape[2]

    def find_gain(start, width):
        def add_states(t, total):
            part = states[
                pl.ds(pl.multiple_of(t * PIECE, PIECE), PIECE), start : start + width
            ]
            return total + jnp.sum(part, axis=0, keepdims=True)

        centre = (
            lax.fori_loop(0, tiles, add_states, jnp.zeros((1, width), jnp.float32))
            / members
        )

        @pl.loop(0, tiles)
        def _(t):
            place = pl.ds(pl.multiple_of(t * PIECE, PIECE), PIECE)
            top, low = split(states[place, start : start + width] - centre)
            state_top[place, :width] = top
            state_low[place, :width] = low

        first = patch * per_device - spread + start // PIECE

        @pl.loop(0, OBS_PER)
        def _(n):
            place = cols(n)
            left_top, left_low = turned_top[place, :], turned_low[place, :]
            right_top, right_low = state_top[:, :width], state_low[:, :width]
            gain = (
                dot(left_top, right_top, PLAIN)
                + dot(left_top, right_low, PLAIN)
                + dot(left_low, right_top, PLAIN)
            ) / (members - 1.0)
            for b in range(width // PIECE):
                at = slice(b * PIECE, (b + 1) * PIECE)
                spot = jnp.clip(first + b, 0, blocks_total - 1)
                top, low = split(gain[:, at] * cover_ref[0, n, spot].astype(jnp.float32))
                gain_top[place, start + b * PIECE : start + (b + 1) * PIECE] = top
                gain_low[place, start + b * PIECE : start + (b + 1) * PIECE] = low

    @pl.loop(0, LOCAL // PIECE)
    def _(i):
        part = cols(i)
        trailing[part, :] = dot(lowered[:, part].T, lowered[...], PLAIN, highest)

    find_gain(edge, edge)
    find_gain(own_width, edge)
    take_states(S_MID, *pieces_of[S_MID])
    find_gain(edge + edge, PIECE)

    @pl.when(has_up)
    def _():
        @pl.when(gives_up)
        def _():
            forward(0).wait_recv()

        @pl.when(is_near)
        def _():
            take_middle(1)

        find_gain(edge + own_width, edge)


    @pl.loop(1, groups)
    def _(k):
        window_copy(W_D, pack.at[1], devs, k).wait_recv()

    @pl.loop(0, members // TILE)
    def _(t):
        place = pl.ds(pl.multiple_of(t * TILE, TILE), TILE)
        top, low = split(dot(devs[place, :], trailing[...], PLAIN, highest))
        weight_top[place, :] = top
        weight_low[place, :] = low

    def increments(start, width, store):
        @pl.loop(0, members // TILE)
        def _(t):
            place = pl.ds(pl.multiple_of(t * TILE, TILE), TILE)
            left_top, left_low = weight_top[place, :], weight_low[place, :]
            right_top = gain_top[:, start : start + width]
            right_low = gain_low[:, start : start + width]
            store(
                place,
                dot(left_top, right_top, PLAIN)
                + dot(left_top, right_low, PLAIN)
                + dot(left_low, right_top, PLAIN),
            )

    def own_part(start, width):
        def store(place, value):
            result[place, start : start + width] = (
                states[place, edge + start : edge + start + width] + value
            )

        increments(edge + start, width, store)

    def other_part(way):
        place_in = (edge + own_width, 0)[way]

        def store(place, value):
            edge_inc[way, place, :] = states[place, place_in : place_in + edge] + value

        increments(place_in, edge, store)

    def foreign(way, owner, b):
        start = (0, own_width - edge)[way]
        bound = offsets_ref[0, owner + way] - owner * per_device
        block = start // PIECE + b
        return at_least(bound, block + 1) if way == 0 else at_least(block, bound)

    half_rows = lower * rows

    def settle(way, b, first=0, last=members):
        start = (0, own_width - edge)[way]
        share = foreign(way, patch, b)
        at = slice(start + b * PIECE, start + (b + 1) * PIECE)

        @pl.loop(first // PIECE, last // PIECE)
        def _(t):
            place = pl.ds(pl.multiple_of(t * PIECE, PIECE), PIECE)
            theirs = edge_got[way, place, b * PIECE : (b + 1) * PIECE]
            result[place, at] = theirs * share + result[place, at] * (1.0 - share)

    def settle_cross(way, owner, first, last):
        @pl.loop(first // PIECE, last // PIECE)
        def _(t):
            place = pl.ds(pl.multiple_of(t * PIECE, PIECE), PIECE)
            for b in range(spread):
                share = foreign(way, owner, b)
                at = slice(b * PIECE, (b + 1) * PIECE)
                mine = edge_inc[way, place, at]
                theirs = cross_got[place, at]
                edge_inc[way, place, at] = mine * share + theirs * (1.0 - share)

    def swap(near_sends, part):
        first = half_rows if near_sends else 0
        count = members - half_rows if near_sends else half_rows
        sent = slice(first, first + count)
        if part == 0:
            way = 0 if near_sends else 1
            source = edge_inc.at[way, sent, :]
            target = edge_got.at[way, sent, :]
        else:
            start = own_width - edge if near_sends else 0
            source = result.at[sent, start : start + edge]
            target = cross_got.at[sent, :]
        return pltpu.make_async_remote_copy(
            src_ref=source,
            dst_ref=target,
            send_sem=pair_send.at[4 + part],
            recv_sem=pair_recv.at[4 + part],
            device_id=(owner_far if near_sends else owner_near, region),
            device_id_type=MESH,
        )

    own_part(edge, PIECE)
    send_back(R_MID, edge, PIECE)
    @pl.when(has_up)
    def _():
        other_part(0)

        @pl.when(gives_up)
        def _():
            for b in range(spread):
                backward(0, b).start()

        @pl.when(is_near)
        def _():
            swap(True, 0).start()

    take_states(S_NEXT, *pieces_of[S_NEXT])
    find_gain(edge + edge + PIECE, middle - PIECE)
    own_part(edge + PIECE, middle - PIECE)
    send_back(R_NEXT, edge + PIECE, middle - PIECE)
    @pl.when(has_dn)
    def _():
        @pl.when(gives_dn)
        def _():
            forward(1).wait_recv()

        @pl.when(is_far)
        def _():
            take_middle(0)

        find_gain(0, edge)
        other_part(1)

        @pl.when(gives_dn)
        def _():
            for b in range(spread):
                backward(1, b).start()

        @pl.when(is_far)
        def _():
            swap(False, 0).start()

    own_part(0, edge)

    @pl.when(is_far)
    def _():
        swap(False, 1).start()

    own_part(own_width - edge, edge)

    @pl.when(is_near)
    def _():
        swap(True, 1).start()

    @pl.when(is_far)
    def _():
        swap(True, 0).wait_recv()

    @pl.when(is_near)
    def _():
        swap(False, 0).wait_recv()

    for b in range(spread):

        @pl.when(gives_dn)
        def _():
            backward(0, b).wait_recv()
            settle(0, b)

        @pl.when(is_far)
        def _():
            settle(0, b, half_rows, members)

        send_back(R_LOW + b, b * PIECE, PIECE)

        @pl.when(gives_up)
        def _():
            backward(1, b).wait_recv()
            settle(1, b)

        @pl.when(is_near)
        def _():
            settle(1, b, 0, half_rows)

        send_back(R_HIGH + b, own_width - edge + b * PIECE, PIECE)

    @pl.when(is_near)
    def _():
        swap(True, 0).wait_send()
        swap(False, 1).wait_recv()
        settle_cross(0, far, 0, half_rows)
        send_cross(0)

    @pl.when(is_far)
    def _():
        swap(False, 0).wait_send()
        swap(True, 1).wait_recv()
        settle_cross(1, near, half_rows, members)
        send_cross(1)

    for copy in halo_copies:
        copy.wait_send()

    @pl.when(gives_dn)
    def _():
        forward(0).wait_send()
        for b in range(spread):
            backward(1, b).wait_send()

    @pl.when(gives_up)
    def _():
        forward(1).wait_send()
        for b in range(spread):
            backward(0, b).wait_send()

    @pl.when(is_near)
    def _():
        swap(True, 1).wait_send()

    @pl.when(is_far)
    def _():
        swap(False, 1).wait_send()

    sent_middle()
    end_cross()

    for slot, (start, width) in pieces_of.items():

        @pl.loop(1, groups)
        def _(k):
            state_copy(slot, start, width, k).wait_send()

    @pl.loop(1, groups)
    def _(k):
        window_copy(W_D, pack.at[1], devs, k).wait_send()

    end_back(R_MID, edge, PIECE)
    end_back(R_NEXT, edge + PIECE, middle - PIECE)
    for b in range(spread):
        end_back(R_LOW + b, b * PIECE, PIECE)
        end_back(R_HIGH + b, own_width - edge + b * PIECE, PIECE)


def body(
    row,
    background_realizations,
    realization_expected_data,
    departure_values,
    instrument_dispersion,
    window_piece_offsets,
    window_data_pieces,
    neighbor_piece_ids,
    coupling_indicator,
):
    groups = lax.axis_size("member")
    regions = lax.axis_size("region")
    rows, variable_total = background_realizations.shape
    obs_width = realization_expected_data.shape[1]
    members = groups * rows
    per_device = variable_total // PIECE // groups
    spread = (per_device - 1) // 2
    own_width = per_device * PIECE
    edge = spread * PIECE
    widest = max(edge, own_width - 2 * edge)
    side = neighbor_piece_ids.shape[-1]
    own_count = obs_width // PIECE
    ext_count = own_count + 2 * side
    f32, bf16 = jnp.float32, jnp.bfloat16
    smem = pl.BlockSpec(memory_space=pltpu.SMEM)
    hbm = pl.BlockSpec(memory_space=pl.ANY)
    return pl.pallas_call(
        functools.partial(analysis_kernel, (groups, regions, row, per_device, spread)),
        out_shape=jax.ShapeDtypeStruct((rows, variable_total), f32),
        in_specs=[smem, smem, smem, smem, hbm, hbm, hbm, pl.BlockSpec(memory_space=pltpu.VMEM)],
        out_specs=hbm,
        scratch_shapes=[
            pltpu.VMEM((rows, obs_width), f32),
            pltpu.VMEM((rows, obs_width), f32),
            pltpu.VMEM((own_count, rows, PIECE), f32),
            pltpu.VMEM((own_count, rows, PIECE), f32),
            pltpu.VMEM((ext_count, rows, PIECE), f32),
            pltpu.VMEM((ext_count, rows, PIECE), f32),
            pltpu.VMEM((own_count, 1, PIECE), f32),
            pltpu.VMEM((ext_count, 1, PIECE), f32),
            pltpu.VMEM((2, 2, side, rows, PIECE), f32),
            pltpu.VMEM((2, side, 1, PIECE), f32),
            pltpu.VMEM((2, members, LOCAL), f32),
            pltpu.VMEM((members, LOCAL), f32),
            pltpu.VMEM((members, LOCAL), f32),
            pltpu.VMEM((members, own_width + 2 * edge), f32),
            pltpu.VMEM((LOCAL, members), f32),
            pltpu.VMEM((LOCAL, members), bf16),
            pltpu.VMEM((LOCAL, members), bf16),
            pltpu.VMEM((LOCAL, LOCAL), f32),
            pltpu.VMEM((PIECE, 2 * PIECE), f32),
            pltpu.VMEM((LOCAL, LOCAL), f32),
            pltpu.VMEM((LOCAL, PIECE), f32),
            pltpu.VMEM((members, LOCAL), bf16),
            pltpu.VMEM((members, LOCAL), bf16),
            pltpu.VMEM((LOCAL, own_width + 2 * edge), bf16),
            pltpu.VMEM((LOCAL, own_width + 2 * edge), bf16),
            pltpu.VMEM((members, widest), bf16),
            pltpu.VMEM((members, widest), bf16),
            pltpu.VMEM((members, own_width), f32),
            pltpu.VMEM((2, members, edge), f32),
            pltpu.VMEM((2, members, edge), f32),
            pltpu.VMEM((members, edge), f32),
            pltpu.SemaphoreType.DMA((10 + 2 * spread, groups)),
            pltpu.SemaphoreType.DMA((10 + 2 * spread, groups)),
            pltpu.SemaphoreType.DMA((6,)),
            pltpu.SemaphoreType.DMA((6,)),
            pltpu.SemaphoreType.DMA((2, spread)),
            pltpu.SemaphoreType.DMA((2, spread)),
            pltpu.SemaphoreType.DMA((3, 2)),
            pltpu.SemaphoreType.DMA((3, 2)),
            pltpu.SemaphoreType.DMA((4,)),
        ],
        compiler_params=pltpu.CompilerParams(
            collective_id=0, has_side_effects=True, vmem_limit_bytes=60 * 1024 * 1024
        ),
        name="analysis",
    )(
        window_data_pieces.swapaxes(1, 2),
        neighbor_piece_ids,
        window_piece_offsets,
        coupling_indicator.swapaxes(1, 2),
        background_realizations,
        realization_expected_data,
        departure_values,
        instrument_dispersion.reshape(-1, PIECE),
    )


def row_length(mesh):
    devices = mesh.devices[:, 0].tolist()
    count = len(devices)
    spots = [getattr(d, "coords", None) for d in devices]
    if any(spot is None for spot in spots):
        return count
    row = 1
    while row < count and spots[row][2] == spots[0][2]:
        row += 1
    return row if count % row == 0 else count


def solution(mesh):
    return jax.shard_map(
        functools.partial(body, row_length(mesh)),
        mesh=mesh,
        in_specs=(
            P("member", "region"),
            P("member", "region"),
            P("member", "region"),
            P("region"),
            P("region", None),
            P("region", None, None),
            P("region", None, None),
            P("region", None, None),
        ),
        out_specs=P("member", "region"),
        check_vma=False,
    )
```

```python
import functools

import jax
import jax.numpy as jnp
from jax import lax
from jax.experimental import pallas as pl
from jax.experimental.pallas import tpu as pltpu
from jax.sharding import PartitionSpec as P

PIECE = 128
OBS_PER = 4
LOCAL = OBS_PER * PIECE
TILE = 256

MESH = pl.DeviceIdType.MESH
highest = lax.Precision.HIGHEST


def cols(start, count=1):
    return pl.ds(pl.multiple_of(start * PIECE, PIECE), count * PIECE)


def dot(left, right, contract, precision=None):
    return lax.dot_general(
        left,
        right,
        ((contract[0], contract[1]), ((), ())),
        precision=precision,
        preferred_element_type=jnp.float32,
    )


def at_least(value, bound):
    return jnp.clip(value - bound + 1, 0, 1).astype(jnp.float32)


PLAIN = ((1,), (0,))
BY_ROWS = ((1,), (1,))


def split(value):
    top = value.astype(jnp.bfloat16)
    return top, (value - top.astype(jnp.float32)).astype(jnp.bfloat16)


def factor_block(block, work_ref):
    size = block.shape[0]
    wide = 2 * size
    eye = lax.broadcasted_iota(jnp.int32, (size, size), 0) == lax.broadcasted_iota(
        jnp.int32, (size, size), 1
    )
    work_ref[:, :size] = block
    work_ref[:, size:] = eye.astype(jnp.float32)
    step_rows = 8
    row_ids = lax.broadcasted_iota(jnp.int32, (step_rows, wide), 0)
    for start in range(0, size, step_rows):
        rows = work_ref[start : start + step_rows, :]
        for j in range(step_rows):
            column = rows[:, start + j : start + j + 1]
            scale = 1.0 / jnp.sqrt(column[j : j + 1, :])
            pivot = rows[j : j + 1, :] * scale
            lowered = rows - (column * scale) * pivot
            rows = jnp.where(row_ids > j, lowered, jnp.where(row_ids == j, pivot, rows))
        work_ref[start : start + step_rows, :] = rows
        after = start + step_rows
        if after < size:
            change = dot(rows[:, :size], rows, ((0,), (0,)), highest)
            work_ref[after:, :] = work_ref[after:, :] - change[after:, :]


def snake(index, row, flip):
    return index + (index // row + flip) % 2 * (row - 1 - 2 * (index % row))


def analysis_kernel(
    plan,
    lists_ref,
    ids_ref,
    offsets_ref,
    cover_ref,
    background,
    expected_hbm,
    innov_hbm,
    flat_var,
    out,
    expected,
    innov,
    own_e,
    own_d,
    ext_e,
    ext_d,
    own_var,
    ext_var,
    halo_send,
    var_send,
    pack,
    obs,
    devs,
    states,
    turned,
    turned_top,
    turned_low,
    trailing,
    work,
    lowered,
    panels,
    weight_top,
    weight_low,
    gain_top,
    gain_low,
    state_top,
    state_low,
    result,
    edge_inc,
    edge_got,
    cross_got,
    member_send,
    member_recv,
    pair_send,
    pair_recv,
    back_send,
    back_recv,
    halo_send_sem,
    halo_recv_sem,
    local_sem,
):
    groups, regions, row, per_device, spread = plan
    rows = expected.shape[0]
    own_count = expected.shape[1] // PIECE
    side = ids_ref.shape[2]
    members = groups * rows
    edge = spread * PIECE
    own_width = per_device * PIECE
    middle = own_width - 2 * edge
    me = lax.axis_index("member")
    region = lax.axis_index("region")
    flip = region % 2
    patch = snake(me, row, flip)
    has_dn = patch > 0
    has_up = patch < groups - 1
    near, far = groups // 2 - 1, groups // 2
    is_near, is_far = patch == near, patch == far
    gives_dn = jnp.logical_and(has_dn, patch != far)
    gives_up = jnp.logical_and(has_up, patch != near)
    owner_near = snake(near, row, flip)
    owner_far = snake(far, row, flip)
    lower = groups // 2
    in_lower = me < lower
    member_dn = snake((patch + groups - 1) % groups, row, flip)
    member_up = snake((patch + 1) % groups, row, flip)
    region_after = (region + 1) % regions
    region_before = (region + regions - 1) % regions
    my_rows = pl.ds(pl.multiple_of(me * rows, rows), rows)

    def rows_of(member):
        return pl.ds(pl.multiple_of(member * rows, rows), rows)

    load_e = pltpu.make_async_copy(expected_hbm, expected, local_sem.at[0])
    load_d = pltpu.make_async_copy(innov_hbm, innov, local_sem.at[1])
    load_e.start()
    load_d.start()

    barrier = pltpu.get_barrier_semaphore()
    for k in range(1, groups):
        pl.semaphore_signal(
            barrier, inc=1, device_id=((me + k) % groups, region), device_id_type=MESH
        )
    for other in (region_after, region_before):
        pl.semaphore_signal(barrier, inc=1, device_id=(me, other), device_id_type=MESH)
    pl.semaphore_wait(barrier, groups + 1)

    def state_copy(slot, start, width, k):
        target = (me + k) % groups
        source = snake(target, row, flip) * own_width + start
        return pltpu.make_async_remote_copy(
            src_ref=background.at[:, pl.ds(pl.multiple_of(source, PIECE), width)],
            dst_ref=states.at[my_rows, edge + start : edge + start + width],
            send_sem=member_send.at[slot, k],
            recv_sem=member_recv.at[slot, k],
            device_id=(target, region),
            device_id_type=MESH,
        )

    def state_own(slot, start, width):
        source = patch * own_width + start
        return pltpu.make_async_copy(
            background.at[:, pl.ds(pl.multiple_of(source, PIECE), width)],
            states.at[my_rows, edge + start : edge + start + width],
            member_recv.at[slot, 0],
        )

    def send_states(slot, start, width):
        @pl.loop(1, groups)
        def _(k):
            state_copy(slot, start, width, k).start()

        state_own(slot, start, width).start()

    def take_states(slot, start, width):
        @pl.loop(1, groups)
        def _(k):
            state_copy(slot, start, width, k).wait_recv()

        state_own(slot, start, width).wait()

    def middle_place(way):
        start = (near * own_width + own_width - edge, far * own_width)[way]
        landing = (0, edge + own_width)[way]
        return (
            background.at[:, start : start + edge],
            states.at[my_rows, landing : landing + edge],
        )

    def middle_copy(way, sender):
        source, target = middle_place(way)
        return pltpu.make_async_remote_copy(
            src_ref=source,
            dst_ref=target,
            send_sem=member_send.at[S_X, way],
            recv_sem=member_recv.at[S_X, sender],
            device_id=((owner_far, owner_near)[way], region),
            device_id_type=MESH,
        )

    def middle_own(way):
        return pltpu.make_async_copy(*middle_place(way), local_sem.at[2])

    def send_middle():
        for way, mine in ((0, is_far), (1, is_near)):

            @pl.when(jnp.logical_not(mine))
            def _():
                middle_copy(way, me).start()

            @pl.when(mine)
            def _():
                middle_own(way).start()

    def sent_middle():
        for way, mine in ((0, is_far), (1, is_near)):

            @pl.when(jnp.logical_not(mine))
            def _():
                middle_copy(way, me).wait_send()

    def take_middle(way):
        @pl.loop(1, groups)
        def _(k):
            middle_copy(way, (me + groups - k) % groups).wait_recv()

        middle_own(way).wait()

    def window_copy(slot, source, target_ref, k):
        return pltpu.make_async_remote_copy(
            src_ref=source.at[rows_of((me + k) % groups), :],
            dst_ref=target_ref.at[my_rows, :],
            send_sem=member_send.at[slot, k],
            recv_sem=member_recv.at[slot, k],
            device_id=((me + k) % groups, region),
            device_id_type=MESH,
        )

    def return_copy(slot, start, width, k):
        return pltpu.make_async_remote_copy(
            src_ref=result.at[rows_of((me + k) % groups), start : start + width],
            dst_ref=out.at[
                :, pl.ds(pl.multiple_of(patch * own_width + start, PIECE), width)
            ],
            send_sem=member_send.at[slot, k],
            recv_sem=member_recv.at[slot, k],
            device_id=((me + k) % groups, region),
            device_id_type=MESH,
        )

    def return_own(slot, start, width):
        return pltpu.make_async_copy(
            result.at[my_rows, start : start + width],
            out.at[:, pl.ds(pl.multiple_of(patch * own_width + start, PIECE), width)],
            member_recv.at[slot, 0],
        )

    def returns(slot, p, member):
        if R_LOW <= slot < R_HIGH:
            return jnp.logical_or(p != far, member >= lower)
        if slot >= R_HIGH:
            return jnp.logical_or(p != near, member < lower)
        return p >= 0

    def send_back(slot, start, width):
        @pl.loop(1, groups)
        def _(k):
            @pl.when(returns(slot, patch, (me + k) % groups))
            def _():
                return_copy(slot, start, width, k).start()

        @pl.when(returns(slot, patch, me))
        def _():
            return_own(slot, start, width).start()

    def end_back(slot, start, width):
        @pl.loop(1, groups)
        def _(k):
            @pl.when(returns(slot, patch, (me + k) % groups))
            def _():
                return_copy(slot, start, width, k).wait_send()

            @pl.when(returns(slot, snake((me + groups - k) % groups, row, flip), me))
            def _():
                return_copy(slot, start, width, k).wait_recv()

        @pl.when(returns(slot, patch, me))
        def _():
            return_own(slot, start, width).wait()

    def cross_place(way, member):
        start = (far * own_width, near * own_width + own_width - edge)[way]
        return (
            edge_inc.at[way, rows_of(member), :],
            out.at[:, start : start + edge],
        )

    def cross_copy(way, member):
        source, target = cross_place(way, member)
        return pltpu.make_async_remote_copy(
            src_ref=source,
            dst_ref=target,
            send_sem=member_send.at[R_X, member],
            recv_sem=member_recv.at[R_X, 0],
            device_id=(member, region),
            device_id_type=MESH,
        )

    def cross_own(way):
        return pltpu.make_async_copy(*cross_place(way, me), local_sem.at[3])

    crossing = ((0, is_near, owner_near, 0, lower), (1, is_far, owner_far, lower, groups))

    def send_cross(way):
        first, last = crossing[way][3:]

        @pl.loop(first, last)
        def _(member):
            @pl.when(member != me)
            def _():
                cross_copy(way, member).start()

        @pl.when(jnp.logical_and(me >= first, me < last))
        def _():
            cross_own(way).start()

    def end_cross():
        for way, mine, owner, first, last in crossing:
            inside = jnp.logical_and(me >= first, me < last)

            @pl.when(mine)
            def _():
                @pl.loop(first, last)
                def _(member):
                    @pl.when(member != me)
                    def _():
                        cross_copy(way, member).wait_send()

                @pl.when(inside)
                def _():
                    cross_own(way).wait()

            @pl.when(jnp.logical_and(inside, me != owner))
            def _():
                cross_copy(way, me).wait_recv()

    S_MID, S_NEXT, S_LOW, S_HIGH, W_E, W_D, S_X, R_X, R_MID, R_NEXT, R_LOW = range(11)
    R_HIGH = R_LOW + spread
    pieces_of = {
        S_MID: (edge, PIECE),
        S_NEXT: (edge + PIECE, middle - PIECE),
        S_LOW: (0, edge),
        S_HIGH: (own_width - edge, edge),
    }

    send_states(S_MID, *pieces_of[S_MID])

    for load, flat, own, ext in (
        (load_e, expected, own_e, ext_e),
        (load_d, innov, own_d, ext_d),
    ):
        load.wait()
        for n in range(own_count):
            block = flat[:, n * PIECE : (n + 1) * PIECE]
            own[n] = block
            ext[n] = block
    for n in range(own_count):
        own_var[n] = flat_var[n : n + 1, :]
        ext_var[n] = flat_var[n : n + 1, :]
    halo_copies = []
    for part, (own, ext, send) in enumerate(
        ((own_e, ext_e, halo_send.at[0]), (own_var, ext_var, var_send), (own_d, ext_d, halo_send.at[1]))
    ):
        for way, other in ((0, region_after), (1, region_before)):
            for k in range(side):
                send[way, k] = own[ids_ref[0, way, k]]
            landing = own_count + way * side
            copy = pltpu.make_async_remote_copy(
                src_ref=send.at[way],
                dst_ref=ext.at[landing : landing + side],
                send_sem=halo_send_sem.at[part, way],
                recv_sem=halo_recv_sem.at[part, way],
                device_id=(me, other),
                device_id_type=MESH,
            )
            copy.start()
            halo_copies.append(copy)

    def pack_window(ext, buffer, k):
        target = (me + k) % groups
        p = snake(target, row, flip)
        for n in range(OBS_PER):
            buffer[rows_of(target), n * PIECE : (n + 1) * PIECE] = ext[lists_ref[0, n, p]]

    for copy in halo_copies[:2]:
        copy.wait_recv()

    @pl.loop(1, groups)
    def _(k):
        pack_window(ext_e, pack.at[0], k)
        window_copy(W_E, pack.at[0], obs, k).start()

    pack_window(ext_e, obs, 0)
    for copy in halo_copies[2:]:
        copy.wait_recv()
    variances = [ext_var[lists_ref[0, n, patch]] for n in range(OBS_PER)]

    @pl.loop(1, groups)
    def _(k):
        pack_window(ext_d, pack.at[1], k)

    pack_window(ext_d, devs, 0)

    @pl.loop(1, groups)
    def _(k):
        window_copy(W_E, pack.at[0], obs, k).wait_send()
        state_copy(S_LOW, *pieces_of[S_LOW], k).start()

    state_own(S_LOW, *pieces_of[S_LOW]).start()
    send_middle()
    send_states(S_HIGH, *pieces_of[S_HIGH])

    @pl.loop(1, groups)
    def _(k):
        window_copy(W_E, pack.at[0], obs, k).wait_recv()

    tiles = members // PIECE

    def add_rows(t, total):
        part = obs[pl.ds(pl.multiple_of(t * PIECE, PIECE), PIECE), :]
        return total + jnp.sum(part, axis=0, keepdims=True)

    mean = lax.fori_loop(0, tiles, add_rows, jnp.zeros((1, LOCAL), jnp.float32)) / members

    @pl.loop(0, tiles)
    def _(t):
        place = pl.ds(pl.multiple_of(t * PIECE, PIECE), PIECE)
        part = obs[place, :] - mean
        obs[place, :] = part
        flat = part.T
        turned[:, place] = flat
        top, low = split(flat)
        turned_top[:, place] = top
        turned_low[:, place] = low

    @pl.loop(0, LOCAL // TILE)
    def _(i):
        place = pl.ds(pl.multiple_of(i * TILE, TILE), TILE)

        @pl.loop(0, LOCAL // TILE)
        def _(j):
            other = pl.ds(pl.multiple_of(j * TILE, TILE), TILE)
            trailing[place, other] = dot(
                turned[place, :], obs[:, other], PLAIN, highest
            ) / (members - 1.0)

    eye = lax.broadcasted_iota(jnp.int32, (PIECE, PIECE), 0) == lax.broadcasted_iota(
        jnp.int32, (PIECE, PIECE), 1
    )
    for n in range(OBS_PER):
        place = slice(n * PIECE, (n + 1) * PIECE)
        trailing[place, place] = trailing[place, place] + jnp.where(eye, variances[n], 0.0)

    def forward(way):
        start, other = ((edge, member_dn), (own_width, member_up))[way]
        landing = (edge + own_width, 0)[way]
        return pltpu.make_async_remote_copy(
            src_ref=states.at[:, start : start + edge],
            dst_ref=states.at[:, landing : landing + edge],
            send_sem=pair_send.at[way],
            recv_sem=pair_recv.at[way],
            device_id=(other, region),
            device_id_type=MESH,
        )

    def backward(way, b):
        other = (member_up, member_dn)[way]
        at = slice(b * PIECE, (b + 1) * PIECE)
        return pltpu.make_async_remote_copy(
            src_ref=edge_inc.at[way, :, at],
            dst_ref=edge_got.at[way, :, at],
            send_sem=back_send.at[way, b],
            recv_sem=back_recv.at[way, b],
            device_id=(other, region),
            device_id_type=MESH,
        )

    line = lax.broadcasted_iota(jnp.int32, (LOCAL, PIECE), 0)
    for n in range(OBS_PER):
        place = slice(n * PIECE, (n + 1) * PIECE)
        lowered[place, :] = jnp.zeros((PIECE, LOCAL), jnp.float32)
        lowered[place, place] = eye.astype(jnp.float32)

    @pl.loop(0, OBS_PER)
    def _(k):
        place = cols(k)
        @pl.when(k == 2)
        def _():
            @pl.loop(1, groups)
            def _(j):
                window_copy(W_D, pack.at[1], devs, j).start()

            take_states(S_LOW, *pieces_of[S_LOW])

            @pl.when(gives_dn)
            def _():
                forward(0).start()

        @pl.when(k == 3)
        def _():
            take_states(S_HIGH, *pieces_of[S_HIGH])

            @pl.when(gives_up)
            def _():
                forward(1).start()

            send_states(S_NEXT, *pieces_of[S_NEXT])

        factor_block(trailing[place, place], work)

        inverse = work[:, PIECE:]
        lowered[place, :] = dot(inverse, lowered[place, :], PLAIN, highest)
        panel = dot(trailing[:, place], inverse, BY_ROWS, highest)
        panel = jnp.where(line >= (k + 1) * PIECE, panel, 0.0)
        panels[...] = panel

        @pl.loop(0, LOCAL // PIECE)
        def _(i):
            part = cols(i)
            trailing[part, :] = trailing[part, :] - dot(
                panels[part, :], panels[...], BY_ROWS, highest
            )
            lowered[part, :] = lowered[part, :] - dot(
                panels[part, :], lowered[place, :], PLAIN, highest
            )

    blocks_total = cover_ref.shape[2]

    def find_gain(start, width):
        def add_states(t, total):
            part = states[
                pl.ds(pl.multiple_of(t * PIECE, PIECE), PIECE), start : start + width
            ]
            return total + jnp.sum(part, axis=0, keepdims=True)

        centre = (
            lax.fori_loop(0, tiles, add_states, jnp.zeros((1, width), jnp.float32))
            / members
        )

        @pl.loop(0, tiles)
        def _(t):
            place = pl.ds(pl.multiple_of(t * PIECE, PIECE), PIECE)
            top, low = split(states[place, start : start + width] - centre)
            state_top[place, :width] = top
            state_low[place, :width] = low

        first = patch * per_device - spread + start // PIECE

        @pl.loop(0, OBS_PER)
        def _(n):
            place = cols(n)
            left_top, left_low = turned_top[place, :], turned_low[place, :]
            right_top, right_low = state_top[:, :width], state_low[:, :width]
            gain = (
                dot(left_top, right_top, PLAIN)
                + dot(left_top, right_low, PLAIN)
                + dot(left_low, right_top, PLAIN)
            ) / (members - 1.0)
            for b in range(width // PIECE):
                at = slice(b * PIECE, (b + 1) * PIECE)
                spot = jnp.clip(first + b, 0, blocks_total - 1)
                top, low = split(gain[:, at] * cover_ref[0, n, spot].astype(jnp.float32))
                gain_top[place, start + b * PIECE : start + (b + 1) * PIECE] = top
                gain_low[place, start + b * PIECE : start + (b + 1) * PIECE] = low

    @pl.loop(0, LOCAL // PIECE)
    def _(i):
        part = cols(i)
        trailing[part, :] = dot(lowered[:, part].T, lowered[...], PLAIN, highest)

    find_gain(edge, edge)
    find_gain(own_width, edge)
    take_states(S_MID, *pieces_of[S_MID])
    find_gain(edge + edge, PIECE)

    @pl.when(has_up)
    def _():
        @pl.when(gives_up)
        def _():
            forward(0).wait_recv()

        @pl.when(is_near)
        def _():
            take_middle(1)

        find_gain(edge + own_width, edge)


    @pl.loop(1, groups)
    def _(k):
        window_copy(W_D, pack.at[1], devs, k).wait_recv()

    @pl.loop(0, members // TILE)
    def _(t):
        place = pl.ds(pl.multiple_of(t * TILE, TILE), TILE)
        top, low = split(dot(devs[place, :], trailing[...], PLAIN, highest))
        weight_top[place, :] = top
        weight_low[place, :] = low

    def increments(start, width, store):
        @pl.loop(0, members // TILE)
        def _(t):
            place = pl.ds(pl.multiple_of(t * TILE, TILE), TILE)
            left_top, left_low = weight_top[place, :], weight_low[place, :]
            right_top = gain_top[:, start : start + width]
            right_low = gain_low[:, start : start + width]
            store(
                place,
                dot(left_top, right_top, PLAIN)
                + dot(left_top, right_low, PLAIN)
                + dot(left_low, right_top, PLAIN),
            )

    def own_part(start, width):
        def store(place, value):
            result[place, start : start + width] = (
                states[place, edge + start : edge + start + width] + value
            )

        increments(edge + start, width, store)

    def other_part(way):
        place_in = (edge + own_width, 0)[way]

        def store(place, value):
            edge_inc[way, place, :] = states[place, place_in : place_in + edge] + value

        increments(place_in, edge, store)

    def foreign(way, owner, b):
        start = (0, own_width - edge)[way]
        bound = offsets_ref[0, owner + way] - owner * per_device
        block = start // PIECE + b
        return at_least(bound, block + 1) if way == 0 else at_least(block, bound)

    half_rows = lower * rows

    def settle(way, b, first=0, last=members):
        start = (0, own_width - edge)[way]
        share = foreign(way, patch, b)
        at = slice(start + b * PIECE, start + (b + 1) * PIECE)

        @pl.loop(first // PIECE, last // PIECE)
        def _(t):
            place = pl.ds(pl.multiple_of(t * PIECE, PIECE), PIECE)
            theirs = edge_got[way, place, b * PIECE : (b + 1) * PIECE]
            result[place, at] = theirs * share + result[place, at] * (1.0 - share)

    def settle_cross(way, owner, first, last):
        @pl.loop(first // PIECE, last // PIECE)
        def _(t):
            place = pl.ds(pl.multiple_of(t * PIECE, PIECE), PIECE)
            for b in range(spread):
                share = foreign(way, owner, b)
                at = slice(b * PIECE, (b + 1) * PIECE)
                mine = edge_inc[way, place, at]
                theirs = cross_got[place, at]
                edge_inc[way, place, at] = mine * share + theirs * (1.0 - share)

    def swap(near_sends, part):
        first = half_rows if near_sends else 0
        count = members - half_rows if near_sends else half_rows
        sent = slice(first, first + count)
        if part == 0:
            way = 0 if near_sends else 1
            source = edge_inc.at[way, sent, :]
            target = edge_got.at[way, sent, :]
        else:
            start = own_width - edge if near_sends else 0
            source = result.at[sent, start : start + edge]
            target = cross_got.at[sent, :]
        return pltpu.make_async_remote_copy(
            src_ref=source,
            dst_ref=target,
            send_sem=pair_send.at[4 + part],
            recv_sem=pair_recv.at[4 + part],
            device_id=(owner_far if near_sends else owner_near, region),
            device_id_type=MESH,
        )

    own_part(edge, PIECE)
    send_back(R_MID, edge, PIECE)
    @pl.when(has_up)
    def _():
        other_part(0)

        @pl.when(gives_up)
        def _():
            for b in range(spread):
                backward(0, b).start()

        @pl.when(is_near)
        def _():
            swap(True, 0).start()

    take_states(S_NEXT, *pieces_of[S_NEXT])
    find_gain(edge + edge + PIECE, middle - PIECE)
    own_part(edge + PIECE, middle - PIECE)
    send_back(R_NEXT, edge + PIECE, middle - PIECE)
    @pl.when(has_dn)
    def _():
        @pl.when(gives_dn)
        def _():
            forward(1).wait_recv()

        @pl.when(is_far)
        def _():
            take_middle(0)

        find_gain(0, edge)
        other_part(1)

        @pl.when(gives_dn)
        def _():
            for b in range(spread):
                backward(1, b).start()

        @pl.when(is_far)
        def _():
            swap(False, 0).start()

    own_part(0, edge)

    @pl.when(is_far)
    def _():
        swap(False, 1).start()

    own_part(own_width - edge, edge)

    @pl.when(is_near)
    def _():
        swap(True, 1).start()

    @pl.when(is_far)
    def _():
        swap(True, 0).wait_recv()

    @pl.when(is_near)
    def _():
        swap(False, 0).wait_recv()

    for b in range(spread):

        @pl.when(gives_dn)
        def _():
            backward(0, b).wait_recv()
            settle(0, b)

        @pl.when(is_far)
        def _():
            settle(0, b, half_rows, members)

        send_back(R_LOW + b, b * PIECE, PIECE)

        @pl.when(gives_up)
        def _():
            backward(1, b).wait_recv()
            settle(1, b)

        @pl.when(is_near)
        def _():
            settle(1, b, 0, half_rows)

        send_back(R_HIGH + b, own_width - edge + b * PIECE, PIECE)

    @pl.when(is_near)
    def _():
        swap(True, 0).wait_send()
        swap(False, 1).wait_recv()
        settle_cross(0, far, 0, half_rows)
        send_cross(0)

    @pl.when(is_far)
    def _():
        swap(False, 0).wait_send()
        swap(True, 1).wait_recv()
        settle_cross(1, near, half_rows, members)
        send_cross(1)

    for copy in halo_copies:
        copy.wait_send()

    @pl.when(gives_dn)
    def _():
        forward(0).wait_send()
        for b in range(spread):
            backward(1, b).wait_send()

    @pl.when(gives_up)
    def _():
        forward(1).wait_send()
        for b in range(spread):
            backward(0, b).wait_send()

    @pl.when(is_near)
    def _():
        swap(True, 1).wait_send()

    @pl.when(is_far)
    def _():
        swap(False, 1).wait_send()

    sent_middle()
    end_cross()

    for slot, (start, width) in pieces_of.items():

        @pl.loop(1, groups)
        def _(k):
            state_copy(slot, start, width, k).wait_send()

    @pl.loop(1, groups)
    def _(k):
        window_copy(W_D, pack.at[1], devs, k).wait_send()

    end_back(R_MID, edge, PIECE)
    end_back(R_NEXT, edge + PIECE, middle - PIECE)
    for b in range(spread):
        end_back(R_LOW + b, b * PIECE, PIECE)
        end_back(R_HIGH + b, own_width - edge + b * PIECE, PIECE)


def body(
    row,
    background_realizations,
    realization_expected_data,
    departure_values,
    instrument_dispersion,
    window_piece_offsets,
    window_data_pieces,
    neighbor_piece_ids,
    coupling_indicator,
):
    groups = lax.axis_size("member")
    regions = lax.axis_size("region")
    rows, variable_total = background_realizations.shape
    obs_width = realization_expected_data.shape[1]
    members = groups * rows
    per_device = variable_total // PIECE // groups
    spread = (per_device - 1) // 2
    own_width = per_device * PIECE
    edge = spread * PIECE
    widest = max(edge, own_width - 2 * edge)
    side = neighbor_piece_ids.shape[-1]
    own_count = obs_width // PIECE
    ext_count = own_count + 2 * side
    f32, bf16 = jnp.float32, jnp.bfloat16
    smem = pl.BlockSpec(memory_space=pltpu.SMEM)
    hbm = pl.BlockSpec(memory_space=pl.ANY)
    return pl.pallas_call(
        functools.partial(analysis_kernel, (groups, regions, row, per_device, spread)),
        out_shape=jax.ShapeDtypeStruct((rows, variable_total), f32),
        in_specs=[smem, smem, smem, smem, hbm, hbm, hbm, pl.BlockSpec(memory_space=pltpu.VMEM)],
        out_specs=hbm,
        scratch_shapes=[
            pltpu.VMEM((rows, obs_width), f32),
            pltpu.VMEM((rows, obs_width), f32),
            pltpu.VMEM((own_count, rows, PIECE), f32),
            pltpu.VMEM((own_count, rows, PIECE), f32),
            pltpu.VMEM((ext_count, rows, PIECE), f32),
            pltpu.VMEM((ext_count, rows, PIECE), f32),
            pltpu.VMEM((own_count, 1, PIECE), f32),
            pltpu.VMEM((ext_count, 1, PIECE), f32),
            pltpu.VMEM((2, 2, side, rows, PIECE), f32),
            pltpu.VMEM((2, side, 1, PIECE), f32),
            pltpu.VMEM((2, members, LOCAL), f32),
            pltpu.VMEM((members, LOCAL), f32),
            pltpu.VMEM((members, LOCAL), f32),
            pltpu.VMEM((members, own_width + 2 * edge), f32),
            pltpu.VMEM((LOCAL, members), f32),
            pltpu.VMEM((LOCAL, members), bf16),
            pltpu.VMEM((LOCAL, members), bf16),
            pltpu.VMEM((LOCAL, LOCAL), f32),
            pltpu.VMEM((PIECE, 2 * PIECE), f32),
            pltpu.VMEM((LOCAL, LOCAL), f32),
            pltpu.VMEM((LOCAL, PIECE), f32),
            pltpu.VMEM((members, LOCAL), bf16),
            pltpu.VMEM((members, LOCAL), bf16),
            pltpu.VMEM((LOCAL, own_width + 2 * edge), bf16),
            pltpu.VMEM((LOCAL, own_width + 2 * edge), bf16),
            pltpu.VMEM((members, widest), bf16),
            pltpu.VMEM((members, widest), bf16),
            pltpu.VMEM((members, own_width), f32),
            pltpu.VMEM((2, members, edge), f32),
            pltpu.VMEM((2, members, edge), f32),
            pltpu.VMEM((members, edge), f32),
            pltpu.SemaphoreType.DMA((10 + 2 * spread, groups)),
            pltpu.SemaphoreType.DMA((10 + 2 * spread, groups)),
            pltpu.SemaphoreType.DMA((6,)),
            pltpu.SemaphoreType.DMA((6,)),
            pltpu.SemaphoreType.DMA((2, spread)),
            pltpu.SemaphoreType.DMA((2, spread)),
            pltpu.SemaphoreType.DMA((3, 2)),
            pltpu.SemaphoreType.DMA((3, 2)),
            pltpu.SemaphoreType.DMA((4,)),
        ],
        compiler_params=pltpu.CompilerParams(
            collective_id=0, has_side_effects=True, vmem_limit_bytes=60 * 1024 * 1024
        ),
        name="analysis",
    )(
        window_data_pieces.swapaxes(1, 2),
        neighbor_piece_ids,
        window_piece_offsets,
        coupling_indicator.swapaxes(1, 2),
        background_realizations,
        realization_expected_data,
        departure_values,
        instrument_dispersion.reshape(-1, PIECE),
    )


def row_length(mesh):
    devices = mesh.devices[:, 0].tolist()
    count = len(devices)
    spots = [getattr(d, "coords", None) for d in devices]
    if any(spot is None for spot in spots):
        return count
    row = 1
    while row < count and spots[row][2] == spots[0][2]:
        row += 1
    return row if count % row == 0 else count


def solution(mesh):
    return jax.shard_map(
        functools.partial(body, row_length(mesh)),
        mesh=mesh,
        in_specs=(
            P("member", "region"),
            P("member", "region"),
            P("member", "region"),
            P("region"),
            P("region", None),
            P("region", None, None),
            P("region", None, None),
            P("region", None, None),
        ),
        out_specs=P("member", "region"),
        check_vma=False,
    )
```
